32 devices in a mesh: head: 4 (over y, x), blk: 8 (over z, core).
Axes of the slice: x: 2, y: 2, z: 4, core: 2. Of those that a mesh axis runs over, the one named last changes fastest.
Arguments:
- queries: bfloat16 [4096, 2048], P(('blk', 'head')), may hold values from -8 to 8
- keys: bfloat16 [4096, 2048], P(('blk', 'head')), may hold values from -8 to 8
- values: bfloat16 [4096, 2048], P(('blk', 'head')), may hold values from -6 to 6
- grad_out: bfloat16 [4096, 2048], P(('blk', 'head')), may hold values from -6 to 6
- stride_owner: int32 [32, 3], replicated, may hold values from 0 to 7, all different within a row; in each aligned block of 4 rows (0 to 3, 4 to 7, ...) at most 2 rows name the same one
Outputs:
- attended: bfloat16 [4096, 2048], P('blk', 'head')
- grad_queries: bfloat16 [4096, 2048], P('blk', 'head')
- grad_keys: bfloat16 [4096, 2048], P('blk', 'head')
- grad_values: bfloat16 [4096, 2048], P('blk', 'head')
The draws below stay inside these ranges and needn't reach their ends.
Inputs may be any that keep to these rules, and one draw needn't show every extreme that they name: `stride_owner`: each row names 3 different runs. Within each aligned block of 4 rows no run is named by more than 2 rows, a bound that some block reaches.
All inputs are finite; a program needn't handle non-finite values.
Results may differ from the reference program's by a relative error of at most 0.02.
Values may be sent and summed in bfloat16 or wider, within the bound.
A program may use at most 128 MiB of HBM per device.

```python
import math
from functools import partial
import jax
import jax.numpy as jnp
import numpy as np
from jax import lax

HEADS = 16
HEAD_DIM = 128
BLOCK = 128
PICKS = 3
STRIDE = 4
QBLOCKS = 32
TOKENS = 4096
CAP = 2
N_BLK = 8


def draw_queries(key, part):
    drawn = jax.random.normal(jax.random.fold_in(key, 1), (TOKENS, HEADS, HEAD_DIM), jnp.float32)
    drawn = jnp.clip(drawn, -6.0, 6.0)
    return drawn.reshape(TOKENS, HEADS * HEAD_DIM).astype(jnp.bfloat16)


def draw_keys(key, part):
    drawn = jax.random.normal(jax.random.fold_in(key, 3), (TOKENS, HEADS, HEAD_DIM), jnp.float32)
    drawn = jnp.clip(drawn, -6.0, 6.0)
    return drawn.reshape(TOKENS, HEADS * HEAD_DIM).astype(jnp.bfloat16)


def block_levels(rng, dims, pieces, low, largest):
    gain = 1.0
    for axis_at, blocks in pieces:
        heights = jax.random.uniform(jax.random.fold_in(jax.random.fold_in(rng, 6), axis_at), (blocks,), jnp.float32, low / len(pieces), largest / len(pieces))
        gain = gain * jnp.repeat(jnp.exp(heights), dims[axis_at] // blocks).reshape((-1,) + (1,) * (len(dims) - 1 - axis_at))
    return gain


def shared_out(stream_key, own, number, rows, count, top, most, skew):
    order = jax.random.permutation(stream_key, count)
    heavy_load, usual = load_shares(count, rows * top, most, skew, True), load_shares(count, rows * top, most, skew, False)
    places = jnp.arange(count)

    def named(sizes, offset_by):
        used = int((sizes > 0).sum())
        fixed = max(1, used // 4)
        moved = fixed + (places - fixed + offset_by * (used - fixed)) % max(1, count - fixed)
        return jnp.zeros((count,), jnp.int32).at[order[jnp.where(places < fixed, places, moved)]].set(jnp.asarray(sizes, jnp.int32))

    sizes = jnp.where(number % 4 == 0, named(heavy_load, number // 4), named(usual, number - number // 4 - 1))
    mixed = jax.random.permutation(jax.random.fold_in(own, 3), count)
    donor, sink = mixed[0:count // 2 * 2:2], mixed[1:count // 2 * 2:2]
    room = jnp.minimum(sizes[donor] - 1, most - sizes[sink]) // 2
    room = jnp.where((donor == order[0]) | (sink == order[0]) | (sizes[sink] == 0), 0, jnp.maximum(room, 0))
    moved = jax.random.randint(jax.random.fold_in(own, 4), (count // 2,), 0, 1 << 20) % (room + 1)
    sizes = sizes.at[donor].add(-moved).at[sink].add(moved)
    labels = jnp.searchsorted(jnp.cumsum(sizes), jnp.arange(rows * top), side="right").astype(jnp.int32)
    listing = labels.reshape(top, rows).T
    listing = listing[jax.random.permutation(jax.random.fold_in(own, 1), rows)]
    offset_by = jax.random.randint(jax.random.fold_in(own, 2), (rows, 1), 0, top)
    return jnp.take_along_axis(listing, (jnp.arange(top)[None, :] + offset_by) % top, axis=1)


def load_shares(number_of, total, limit, skew, full):
    portions = [(1 << 20) // math.isqrt(rank ** skew) + 1 for rank in range(1, number_of + 1)]
    largest = limit if full else min(limit, max(-(-total // number_of), total * portions[0] // sum(portions)))
    least = 1 if total - largest >= number_of - 1 else 0
    holding, rest = [largest] + [least] * (number_of - 1), total - largest - least * (number_of - 1)
    while rest > 0:
        candidates = [i for i in range(1, number_of) if holding[i] < largest] or [i for i in range(1, number_of) if holding[i] < limit]
        whole, remaining = sum([portions[i] for i in candidates]), rest
        for i in candidates:
            addition = min(limit - holding[i], max(1, remaining * portions[i] // whole), rest)
            holding[i] = holding[i] + addition
            rest = rest - addition
    return np.array(holding)


def noise(stream_key, shape, deviation, most, pieces=(), kind=jnp.bfloat16):
    array = jax.random.normal(stream_key, shape, jnp.float32) * deviation
    if len(pieces) > 0:
        array = block_levels(stream_key, shape, pieces, -0.22, 0.18) * array
    return jnp.clip(array, min=-most, max=most).astype(kind)


def setup_inputs(seed: int = 0) -> dict:
    streams_of = jax.random.split(jax.random.key(seed), 6)
    queries = draw_queries(jax.random.fold_in(streams_of[5], 71), 0)
    keys = draw_keys(jax.random.fold_in(streams_of[5], 71), 0)
    values = noise(streams_of[2], (TOKENS, HEADS * HEAD_DIM), 1.0, 6.0, ((0, 32),))
    grad_out = noise(streams_of[3], (TOKENS, HEADS * HEAD_DIM), 1.0, 6.0, ((0, 32),))
    stride_owner_keys = jax.random.split(jax.random.fold_in(streams_of[4], 1), QBLOCKS // STRIDE)
    stride_owner_turns = jax.random.permutation(jax.random.fold_in(streams_of[4], 3), QBLOCKS // STRIDE)
    stride_owner = jax.vmap(lambda own, number: shared_out(jax.random.fold_in(streams_of[4], 2), own, number, STRIDE, N_BLK, PICKS, CAP, 2))(stride_owner_keys, stride_owner_turns).reshape((QBLOCKS, PICKS))
    return dict(queries=queries, keys=keys, values=values, grad_out=grad_out, stride_owner=stride_owner)


def to_bf16_wide(source):
    return lax.optimization_barrier(source.astype(jnp.bfloat16)).astype(jnp.float32)


def key_table(stride_owner):
    blocks = jnp.arange(QBLOCKS, dtype=jnp.int32)
    offset = (blocks % STRIDE).astype(jnp.int32)
    strided = (stride_owner.astype(jnp.int32) * STRIDE + offset[:, None]).astype(jnp.int32)
    nearby = jnp.stack([(blocks - 1) % QBLOCKS, blocks, (blocks + 1) % QBLOCKS], axis=1).astype(jnp.int32)
    leading = jnp.zeros((QBLOCKS, 2), jnp.int32) + jnp.arange(2, dtype=jnp.int32)[None, :]
    return jnp.concatenate([nearby, strided, leading], axis=1).astype(jnp.int32)


def settle(terms):
    rounded = to_bf16_wide(terms[:, 3:6])
    return jnp.concatenate([terms[:, :3], rounded, terms[:, 6:]], axis=1)


def head_pass(table, operands):
    query_head, key_head, value_head, grad_head = operands
    factor = HEAD_DIM ** -0.5
    key_sets = key_head[table].astype(jnp.float32)
    value_sets = value_head[table].astype(jnp.float32)
    query_wide = query_head.astype(jnp.float32)
    grad_wide = grad_head.astype(jnp.float32)
    scores = jnp.einsum('iqd,ijkd->iqjk', query_wide, key_sets) * factor
    row_max = jnp.max(scores, axis=(2, 3), keepdims=True)
    log_total = row_max + jnp.log(jnp.sum(jnp.exp(scores - row_max), axis=(2, 3), keepdims=True))
    weights = jnp.exp(scores - log_total)
    rounded = to_bf16_wide(weights)
    attended = jnp.einsum('iqjk,ijkd->iqd', rounded, value_sets).astype(jnp.bfloat16)
    grad_weights = jnp.einsum('iqd,ijkd->iqjk', grad_wide, value_sets)
    delta = jnp.sum(grad_wide * attended.astype(jnp.float32), axis=-1)[:, :, None, None]
    grad_scores = to_bf16_wide(weights * (grad_weights - delta) * factor)
    grad_queries = jnp.einsum('iqjk,ijkd->iqd', grad_scores, key_sets).astype(jnp.bfloat16)
    key_terms = settle(jnp.einsum('iqjk,iqd->ijkd', grad_scores, query_wide))
    value_terms = settle(jnp.einsum('iqjk,iqd->ijkd', rounded, grad_wide))
    blank = jnp.zeros((QBLOCKS, BLOCK, HEAD_DIM), jnp.float32)
    grad_keys = blank.at[table].add(key_terms).astype(jnp.bfloat16)
    grad_values = blank.at[table].add(value_terms).astype(jnp.bfloat16)
    return attended, grad_queries, grad_keys, grad_values


def per_head(source):
    return source.reshape(QBLOCKS, BLOCK, HEADS, HEAD_DIM).transpose(2, 0, 1, 3)


def back_rows(source):
    return source.transpose(1, 2, 0, 3).reshape(TOKENS, HEADS * HEAD_DIM)


def reference(queries, keys, values, grad_out, stride_owner):
    table = key_table(stride_owner)
    results = lax.map(partial(head_pass, table), (per_head(queries), per_head(keys), per_head(values), per_head(grad_out)))
    return back_rows(results[0]), back_rows(results[1]), back_rows(results[2]), back_rows(results[3])
```

```python
import math
from functools import partial

import jax
import jax.numpy as jnp
from jax import lax
from jax.experimental import pallas as pl
from jax.experimental.pallas import tpu as pltpu
from jax.sharding import PartitionSpec as P

HEAD_DIM = 128
BLOCK = 128
PICKS = 3
MESH = pl.DeviceIdType.MESH


def with_halo(block, sides, width):
    for axis, dim in sides:
        count = lax.axis_size(axis)
        forward = [(i, i + 1) for i in range(count - 1)]
        forward.append((count - 1, 0))
        backward = [(target, source) for source, target in forward]
        low = lax.ppermute(
            lax.slice_in_dim(block, block.shape[dim] - width, None, axis=dim), axis, forward
        )
        high = lax.ppermute(lax.slice_in_dim(block, 0, width, axis=dim), axis, backward)
        block = jnp.concatenate([low, block, high], axis=dim)
    return block


def from_root(block, axis, holder):
    block = jnp.where(lax.axis_index(axis) == holder, block, jnp.zeros_like(block))
    return lax.psum(block, axis)


def slot_tables(stride_owner, n_blk, blocks, capacity, device):
    owner_table = stride_owner.reshape(n_blk, blocks, PICKS)
    owner_ids = jnp.arange(n_blk, dtype=jnp.int32)
    naming = jnp.any(owner_table[:, :, :, None] == owner_ids[None, None, None, :], axis=2)
    counts = naming.astype(jnp.int32)
    ranking = jnp.cumsum(counts, axis=1) - counts
    naming_here = lax.dynamic_index_in_dim(naming, device, 2, keepdims=False)
    ranking_here = lax.dynamic_index_in_dim(ranking, device, 2, keepdims=False)
    slot_ids = jnp.arange(capacity, dtype=jnp.int32)
    matched = naming_here[:, None, :] & (ranking_here[:, None, :] == slot_ids[None, :, None])
    offsets = jnp.sum(
        matched.astype(jnp.int32) * jnp.arange(blocks, dtype=jnp.int32)[None, None, :], axis=2
    )
    own_rows = lax.dynamic_index_in_dim(owner_table, device, 0, keepdims=False)
    own_ranks = lax.dynamic_index_in_dim(ranking, device, 0, keepdims=False)
    picked = jnp.take_along_axis(own_ranks, own_rows, axis=1)
    flat_slot = own_rows * capacity + picked
    return (offsets.reshape(-1), flat_slot, matched.reshape(n_blk * capacity, blocks))


def fetch_keys(stacked, offsets, flat_slot, capacity):
    seq_rows = stacked.shape[1]
    width = stacked.shape[2]
    blocks = seq_rows // BLOCK
    n_blk = lax.axis_size("blk")
    extended = with_halo(stacked, (("blk", 1),), BLOCK)
    extended = extended.reshape(2, blocks + 2, BLOCK, width)
    block_view = stacked.reshape(2, blocks, BLOCK, width)
    leading = from_root(block_view[:, 0:2], "blk", 0)
    outgoing = jnp.take(block_view, offsets, axis=1).reshape(2, n_blk, capacity, BLOCK, width)
    incoming = lax.all_to_all(outgoing, "blk", split_axis=1, concat_axis=1, tiled=True)
    incoming = incoming.reshape(2, n_blk * capacity, BLOCK, width)
    pooled = jnp.concatenate([extended, incoming, leading], axis=1)
    rows_here = jnp.arange(blocks, dtype=jnp.int32)[:, None]
    nearby_index = rows_here + jnp.arange(3, dtype=jnp.int32)[None, :]
    distant_index = blocks + 2 + flat_slot
    leading_index = (
        jnp.zeros((blocks, 2), jnp.int32)
        + (blocks + 2 + n_blk * capacity)
        + jnp.arange(2, dtype=jnp.int32)[None, :]
    )
    table = jnp.concatenate([nearby_index, distant_index, leading_index], axis=1)
    return jnp.take(pooled, table.reshape(-1), axis=1)


def score_block(query_part, key_part, factor):
    return (
        jnp.einsum("gqhd,gjkhd->ghqjk", query_part, key_part, preferred_element_type=jnp.float32)
        * factor
    )


def log_normal(scores):
    row_max = jnp.max(scores, axis=(3, 4), keepdims=True)
    return row_max + jnp.log(jnp.sum(jnp.exp(scores - row_max), axis=(3, 4), keepdims=True))


def output_of(rounded, value_part):
    return jnp.einsum(
        "ghqjk,gjkhd->gqhd", rounded, value_part, preferred_element_type=jnp.float32
    ).astype(jnp.bfloat16)


def split_terms(coeffs, source):
    group_size = source.shape[0]
    near = jnp.einsum(
        "ghqjk,gqhd->gjkhd", coeffs[:, :, :, 0:3], source, preferred_element_type=jnp.float32
    )
    far = jnp.einsum(
        "ghqjk,gqhd->gjkhd", coeffs[:, :, :, 3:6], source, preferred_element_type=jnp.float32
    ).astype(jnp.bfloat16)
    lead = jnp.einsum(
        "ghqjk,gqhd->jkhd", coeffs[:, :, :, 6:8], source, preferred_element_type=jnp.float32
    )
    near = near.reshape(group_size, 3, near.shape[2], near.shape[3] * near.shape[4])
    far = far.reshape(group_size, 3, far.shape[2], far.shape[3] * far.shape[4])
    lead = lead.reshape(2, lead.shape[1], lead.shape[2] * lead.shape[3])
    return (near, far, lead)


def backward_from(
    scores, log_total, rounded, attended, grad_part, query_part, key_part, value_part, factor
):
    grad_weights = jnp.einsum(
        "gqhd,gjkhd->ghqjk", grad_part, value_part, preferred_element_type=jnp.float32
    )
    delta = jnp.sum(grad_part.astype(jnp.float32) * attended.astype(jnp.float32), axis=3)
    delta = jnp.transpose(delta, (0, 2, 1))[:, :, :, None, None]
    grad_scores = (jnp.exp(scores - log_total) * (grad_weights - delta) * factor).astype(
        jnp.bfloat16
    )
    grad_query = jnp.einsum(
        "ghqjk,gjkhd->gqhd", grad_scores, key_part, preferred_element_type=jnp.float32
    ).astype(jnp.bfloat16)
    key_near, key_far, key_lead = split_terms(grad_scores, query_part)
    value_near, value_far, value_lead = split_terms(rounded, grad_part)
    return (grad_query, key_near, key_far, key_lead, value_near, value_far, value_lead)


def spread_near(near_terms, width):
    blank = jnp.zeros((1, BLOCK, width), jnp.float32)
    return (
        jnp.concatenate([near_terms[:, 0], blank, blank], axis=0)
        + jnp.concatenate([blank, near_terms[:, 1], blank], axis=0)
        + jnp.concatenate([blank, blank, near_terms[:, 2]], axis=0)
    )


def by_runs(queries, keys, values, grad_out, stride_owner):
    query_rows, key_rows, value_rows, grad_rows = (
        lax.all_to_all(queries, "head", split_axis=1, concat_axis=0, tiled=True),
        lax.all_to_all(keys, "head", split_axis=1, concat_axis=0, tiled=True),
        lax.all_to_all(values, "head", split_axis=1, concat_axis=0, tiled=True),
        lax.all_to_all(grad_out, "head", split_axis=1, concat_axis=0, tiled=True),
    )
    seq_rows, width = query_rows.shape
    heads_here = width // HEAD_DIM
    blocks = seq_rows // BLOCK
    n_blk = lax.axis_size("blk")
    capacity = max(2, (PICKS * blocks + n_blk - 1) // n_blk)
    device = lax.axis_index("blk")
    offsets, flat_slot, matched = slot_tables(stride_owner, n_blk, blocks, capacity, device)
    group_size = math.gcd(blocks, max(1, 512 // BLOCK))
    group_count = blocks // group_size
    factor = HEAD_DIM ** (-0.5)
    stacked = jnp.stack([key_rows, value_rows])
    query_view = query_rows.reshape(blocks, BLOCK, heads_here, HEAD_DIM)
    grad_view = grad_rows.reshape(blocks, BLOCK, heads_here, HEAD_DIM)
    key_sets = fetch_keys(stacked, offsets, flat_slot, capacity)
    key_sets = key_sets.reshape(2, blocks, 8, BLOCK, heads_here, HEAD_DIM)

    def pieces(group_id):
        start = group_id * group_size
        query_part = lax.dynamic_slice_in_dim(query_view, start, group_size, 0)
        grad_part = lax.dynamic_slice_in_dim(grad_view, start, group_size, 0)
        kv_part = lax.dynamic_slice_in_dim(key_sets, start, group_size, 1)
        return (query_part, grad_part, kv_part[0], kv_part[1])

    def joined_pass(group_id):
        query_part, grad_part, key_part, value_part = pieces(group_id)
        scores = score_block(query_part, key_part, factor)
        log_total = log_normal(scores)
        rounded = jnp.exp(scores - log_total).astype(jnp.bfloat16)
        attended = output_of(rounded, value_part)
        extra = backward_from(
            scores,
            log_total,
            rounded,
            attended,
            grad_part,
            query_part,
            key_part,
            value_part,
            factor,
        )
        return (attended,) + extra

    group_ids = jnp.arange(group_count, dtype=jnp.int32)
    results = lax.map(joined_pass, group_ids)
    attended = results[0]
    grad_query, key_near, key_far, key_lead, value_near, value_far, value_lead = results[1:]
    key_ext = spread_near(key_near.reshape(blocks, 3, BLOCK, width), width)
    value_ext = spread_near(value_near.reshape(blocks, 3, BLOCK, width), width)
    rim_terms = jnp.stack(
        [
            jnp.stack([key_ext[0], value_ext[0]]),
            jnp.stack([key_ext[blocks + 1], value_ext[blocks + 1]]),
        ]
    )
    beside = with_halo(rim_terms.astype(jnp.bfloat16), (("blk", 0),), 1).astype(rim_terms.dtype)
    key_owned = key_ext[1 : blocks + 1].at[0].add(beside[0, 0]).at[blocks - 1].add(beside[3, 0])
    value_owned = value_ext[1 : blocks + 1].at[0].add(beside[0, 1]).at[blocks - 1].add(beside[3, 1])
    slot_flat = flat_slot.reshape(-1)
    key_back = (
        jnp.zeros((n_blk * capacity, BLOCK, width), jnp.bfloat16)
        .at[slot_flat]
        .set(key_far.reshape(blocks * PICKS, BLOCK, width))
    )
    value_back = (
        jnp.zeros((n_blk * capacity, BLOCK, width), jnp.bfloat16)
        .at[slot_flat]
        .set(value_far.reshape(blocks * PICKS, BLOCK, width))
    )
    key_arrived, value_arrived = (
        lax.all_to_all(
            key_back.reshape(n_blk, capacity, BLOCK, width),
            "blk",
            split_axis=0,
            concat_axis=0,
            tiled=True,
        ),
        lax.all_to_all(
            value_back.reshape(n_blk, capacity, BLOCK, width),
            "blk",
            split_axis=0,
            concat_axis=0,
            tiled=True,
        ),
    )
    match_b = matched.astype(jnp.bfloat16)
    key_owned = key_owned + jnp.einsum(
        "sr,sbc->rbc",
        match_b,
        key_arrived.reshape(n_blk * capacity, BLOCK, width),
        preferred_element_type=jnp.float32,
    )
    value_owned = value_owned + jnp.einsum(
        "sr,sbc->rbc",
        match_b,
        value_arrived.reshape(n_blk * capacity, BLOCK, width),
        preferred_element_type=jnp.float32,
    )
    key_total, value_total = (
        lax.psum(jnp.sum(key_lead, axis=0).astype(jnp.bfloat16), "blk").astype(jnp.float32),
        lax.psum(jnp.sum(value_lead, axis=0).astype(jnp.bfloat16), "blk").astype(jnp.float32),
    )
    at_root = device == 0
    key_owned = key_owned.at[0:2].add(jnp.where(at_root, key_total, jnp.zeros_like(key_total)))
    value_owned = value_owned.at[0:2].add(
        jnp.where(at_root, value_total, jnp.zeros_like(value_total))
    )
    grad_keys = key_owned.astype(jnp.bfloat16).reshape(seq_rows, width)
    grad_values = value_owned.astype(jnp.bfloat16).reshape(seq_rows, width)
    return (
        attended.reshape(seq_rows, width),
        grad_query.reshape(seq_rows, width),
        grad_keys,
        grad_values,
    )


def head_kernel(
    n_head,
    n_z,
    owner_in,
    q_in,
    k_in,
    v_in,
    g_in,
    out,
    owner_ref,
    kv_all,
    qg_all,
    k_sum,
    v_sum,
    k_far,
    v_far,
    stage,
    give,
    take,
    owner_sem,
    kv_send,
    kv_recv,
    qg_send,
    qg_recv,
    pass_send,
    pass_recv,
    pair_send,
    pair_recv,
    row_send,
    key_send,
    out_recv,
    near_sem,
):
    head = lax.axis_index("head")
    blk = lax.axis_index("blk")
    z = blk // 2
    c = blk % 2
    runs = n_head
    total_blocks = 2 * n_z * runs
    factor = HEAD_DIM ** (-0.5)
    my_head = head * n_z + z
    mine = blk * runs + head
    my_row = z * runs + head
    sibling = {"head": head, "blk": 2 * z + 1 - c}

    def columns(head_id):
        return pl.ds(pl.multiple_of(head_id * HEAD_DIM, HEAD_DIM), HEAD_DIM)

    bits = [1 << b for b in range(n_head.bit_length() - 1)]

    def greet(sem):
        for flip in bits:
            pl.semaphore_signal(
                sem,
                inc=1,
                device_id={"head": flipped(head, flip), "blk": blk},
                device_id_type=MESH,
            )
        pl.semaphore_signal(sem, inc=1, device_id=sibling, device_id_type=MESH)

        @pl.when(z > 0)
        def _():
            pl.semaphore_signal(
                sem, inc=1, device_id={"head": head, "blk": blk - 2}, device_id_type=MESH
            )

        @pl.when(z < n_z - 1)
        def _():
            pl.semaphore_signal(
                sem, inc=1, device_id={"head": head, "blk": blk + 2}, device_id_type=MESH
            )

    def flipped(head_id, flips):
        moved = head_id
        for flip in bits:
            if flips & flip:
                moved = moved + flip - 2 * flip * ((head_id // flip) % 2)
        return moved

    def hear(sem):
        ends = len(bits) + 1 + (z > 0).astype(jnp.int32) + (z < n_z - 1).astype(jnp.int32)
        pl.semaphore_wait(sem, ends)

    barrier = pltpu.get_barrier_semaphore()
    greet(barrier)

    local = [pltpu.make_async_copy(owner_in, owner_ref, owner_sem.at[0])]
    for at, source in enumerate((k_in, v_in)):
        local.append(
            pltpu.make_async_copy(
                source.at[:, columns(my_head)], kv_all.at[at, mine], kv_recv.at[0]
            )
        )
    for at, source in enumerate((q_in, g_in)):
        local.append(
            pltpu.make_async_copy(
                source.at[:, columns(my_head)], qg_all.at[at, my_row], qg_recv.at[0]
            )
        )
    for copy in local:
        copy.start()

    def push(at, source, target, slot, send_sem, recv_sem, z2, flips):
        h2 = flipped(head, flips)
        pltpu.make_async_remote_copy(
            src_ref=source.at[:, columns(h2 * n_z + z2)],
            dst_ref=target.at[at, slot],
            send_sem=send_sem.at[0],
            recv_sem=recv_sem,
            device_id={"head": h2, "blk": 2 * z2 + c},
            device_id_type=MESH,
        ).start()

    def push_pair(sources, target, slot, send_sem, recv_sem, dz, flips):
        for sign in (1, -1) if dz else (1,):
            z2 = z + sign * dz

            @pl.when((z2 >= 0) & (z2 < n_z))
            def _(z2=z2):
                arrive = recv_sem.at[(z2 + n_z - z) % n_z]
                for at, source in enumerate(sources):
                    push(at, source, target, slot, send_sem, arrive, z2, flips)

    def hops(flips):
        return sum(1 for flip in bits if flips & flip)

    everyone = sorted(
        (dz + hops(flips), -dz, flips)
        for dz in range(n_z)
        for flips in range(n_head)
        if dz + hops(flips) > 0
    )
    rounds = n_z - 1 + len(bits)
    for distance in range(1, rounds + 1):
        if distance == 1:
            hear(barrier)
        else:
            hear(near_sem.at[distance - 2])
        if distance < rounds:
            greet(near_sem.at[distance - 1])
        for hop, minus, flips in everyone:
            if hop == distance:
                push_pair((k_in, v_in), kv_all, mine, kv_send, kv_recv, -minus, flips)
    for dz in [n_z // 2] + [d for d in range(n_z - 1, -1, -1) if d != n_z // 2]:
        for flips in range(n_head):
            if dz + hops(flips) > 0:
                push_pair((q_in, g_in), qg_all, my_row, qg_send, qg_recv, dz, flips)

    blank = jnp.zeros((BLOCK, HEAD_DIM), jnp.float32)

    def clear(n, carry):
        k_sum[n] = blank
        v_sum[n] = blank
        return carry

    lax.fori_loop(0, total_blocks, clear, 0)
    none = n_z * runs * PICKS
    k_far[none] = blank.astype(jnp.bfloat16)
    v_far[none] = blank.astype(jnp.bfloat16)

    def await_bytes(ref, sem):
        pltpu.make_async_remote_copy(
            src_ref=ref,
            dst_ref=ref,
            send_sem=sem,
            recv_sem=sem,
            device_id=sibling,
            device_id_type=MESH,
        ).wait_recv()

    def run_of(dz, core):
        return 2 * ((z + n_z - dz) % n_z) + core

    passes = []
    order = [0, 1, n_z - 1] + list(range(2, n_z - 1))
    for dz in order[:n_z]:
        group = kv_all.at[:, pl.ds(run_of(dz, c) * runs, runs)]
        await_bytes(group, kv_recv.at[dz])
        copy = pltpu.make_async_remote_copy(
            src_ref=group,
            dst_ref=group,
            send_sem=pass_send.at[dz],
            recv_sem=pass_recv.at[dz],
            device_id=sibling,
            device_id_type=MESH,
        )
        copy.start()
        passes.append(copy)
    local[0].wait()
    for dz in range(n_z):
        await_bytes(kv_all.at[:, pl.ds(run_of(dz, 1 - c) * runs, runs)], pass_recv.at[dz])

    def contract(left, right, dims):
        return lax.dot_general(
            left, right, ((dims[:1], dims[1:]), ((), ())), preferred_element_type=jnp.float32
        )

    def query_step(z1, r):
        row = z1 * runs + r
        block = (2 * z1 + c) * runs + r
        low = (block + total_blocks - 1) % total_blocks
        high = (block + 1) % total_blocks
        picks = [owner_ref[j, block] * runs + r for j in range(PICKS)]
        named = [low, block, high] + picks + [0, 1]
        keys = jnp.concatenate([kv_all[0, n] for n in named], axis=0)
        values = jnp.concatenate([kv_all[1, n] for n in named], axis=0)
        query = qg_all[0, row]
        grad = qg_all[1, row]
        scores = contract(keys, query, (1, 1))
        top = jnp.max(scores, axis=0, keepdims=True)
        weights = jnp.exp((scores - top) * factor)
        weights = weights * (1.0 / jnp.sum(weights, axis=0, keepdims=True))
        rounded = weights.astype(jnp.bfloat16)
        grad_weights = contract(values, grad, (1, 1))
        delta = jnp.sum(weights * grad_weights, axis=0, keepdims=True)
        grad_scores = (weights * (grad_weights - delta) * factor).astype(jnp.bfloat16)
        stage[0, row] = contract(rounded, values, (0, 0)).astype(jnp.bfloat16)
        stage[1, row] = contract(grad_scores, keys, (0, 0)).astype(jnp.bfloat16)
        key_terms = contract(grad_scores, query, (1, 0))
        value_terms = contract(rounded, grad, (1, 0))
        for j, n in ((0, low), (1, block), (2, high), (6, 0), (7, 1)):
            k_sum[n] += key_terms[j * BLOCK : (j + 1) * BLOCK]
            v_sum[n] += value_terms[j * BLOCK : (j + 1) * BLOCK]
        for j in range(PICKS):
            rows = slice((3 + j) * BLOCK, (4 + j) * BLOCK)
            k_far[row * PICKS + j] = key_terms[rows].astype(jnp.bfloat16)
            v_far[row * PICKS + j] = value_terms[rows].astype(jnp.bfloat16)

    def hand_out(first, send_sem, dz):
        z2 = (z + n_z - dz) % n_z
        source = stage.at[pl.ds(first, 2), pl.ds(z2 * runs, runs)]
        target = out.at[pl.ds(first, 2), :, :, columns(z)]
        if dz == 0:
            pltpu.make_async_copy(source, target, out_recv.at[0]).start()
        else:
            pltpu.make_async_remote_copy(
                src_ref=source,
                dst_ref=target,
                send_sem=send_sem.at[0],
                recv_sem=out_recv.at[0],
                device_id={"head": head, "blk": 2 * z2 + c},
                device_id_type=MESH,
            ).start()

    far_first = [dz for dz in (2, 1, 3, 0) if dz < n_z] + list(range(4, n_z))
    for dz in far_first:
        z1 = (z + n_z - dz) % n_z
        await_bytes(qg_all.at[:, pl.ds(z1 * runs, runs)], qg_recv.at[dz])

        def step(r, carry, z1=z1):
            query_step(z1, r)
            return carry

        lax.fori_loop(0, runs, step, 0)
        hand_out(0, row_send, dz)

    def total_of(sums, far, run, r):
        total = sums[run * runs + r]
        for z1 in range(n_z):
            block = (2 * z1 + c) * runs + r
            row = z1 * runs + r
            place = none
            for j in range(PICKS):
                place = jnp.where(owner_ref[j, block] == run, row * PICKS + j, place)
            total = total + far[place].astype(jnp.float32)
        return total

    def give_step(row, carry):
        run, r = 2 * (row // runs) + 1 - c, row % runs
        give[0, row] = total_of(k_sum, k_far, run, r).astype(jnp.bfloat16)
        give[1, row] = total_of(v_sum, v_far, run, r).astype(jnp.bfloat16)
        return carry

    lax.fori_loop(0, n_z * runs, give_step, 0)
    pair = pltpu.make_async_remote_copy(
        src_ref=give,
        dst_ref=take,
        send_sem=pair_send.at[0],
        recv_sem=pair_recv.at[0],
        device_id=sibling,
        device_id_type=MESH,
    )
    pair.start()
    pair.wait_recv()
    for dz in far_first:
        z1 = (z + n_z - dz) % n_z

        def join_step(r, carry, z1=z1):
            row, run = z1 * runs + r, 2 * z1 + c
            for at, sums, far in ((0, k_sum, k_far), (1, v_sum, v_far)):
                total = total_of(sums, far, run, r) + take[at, row].astype(jnp.float32)
                stage[2 + at, row] = total.astype(jnp.bfloat16)
            return carry

        lax.fori_loop(0, runs, join_step, 0)
        hand_out(2, key_send, dz)

    def await_sent(ref, sem):
        pltpu.make_async_remote_copy(
            src_ref=ref,
            dst_ref=ref,
            send_sem=sem,
            recv_sem=sem,
            device_id=sibling,
            device_id_type=MESH,
        ).wait_send()

    rows = n_z * runs
    for copy in passes + [pair]:
        copy.wait_send()
    await_sent(kv_all.at[:, pl.ds(0, rows - 1)], kv_send.at[0])
    await_sent(qg_all.at[:, pl.ds(0, rows - 1)], qg_send.at[0])
    if n_z > 1:
        for send_sem in (row_send, key_send):
            await_sent(qg_all.at[:, pl.ds(0, rows - runs)], send_sem.at[0])
    await_bytes(out, out_recv.at[0])


def settle_kernel(count, pieces, source, *refs):
    targets, sem = refs[:count], refs[count]
    copies = [
        pltpu.make_async_copy(
            source.at[at, piece], targets[at].at[piece], sem.at[at * pieces + piece]
        )
        for at in range(count)
        for piece in range(pieces)
    ]
    for copy in copies:
        copy.start()
    for copy in copies:
        copy.wait()


def by_heads(queries, keys, values, grad_out, stride_owner):
    n_head, n_blk = lax.axis_size("head"), lax.axis_size("blk")
    n_z = n_blk // 2
    rows = n_z * n_head
    rounds = n_z - 1 + n_head.bit_length() - 1
    seq_rows, width = BLOCK * n_head, n_z * HEAD_DIM
    tile = (BLOCK, HEAD_DIM)
    low, wide = jnp.bfloat16, jnp.float32
    dma = pltpu.SemaphoreType.DMA
    out_bytes = 8 * seq_rows * width
    arrived = pl.pallas_call(
        partial(head_kernel, n_head, n_z),
        out_shape=pltpu.VMEM((4, n_head, BLOCK, width), low),
        in_specs=[pl.BlockSpec(memory_space=pltpu.HBM)] * 5,
        out_specs=pl.BlockSpec(memory_space=pltpu.VMEM),
        scratch_shapes=[
            pltpu.SMEM(stride_owner.shape[::-1], jnp.int32),
            pltpu.VMEM((2, 2 * rows) + tile, low),
            pltpu.VMEM((2, rows) + tile, low),
            pltpu.VMEM((2 * rows,) + tile, wide),
            pltpu.VMEM((2 * rows,) + tile, wide),
            pltpu.VMEM((rows * PICKS + 1,) + tile, low),
            pltpu.VMEM((rows * PICKS + 1,) + tile, low),
            pltpu.VMEM((4, rows) + tile, low),
            pltpu.VMEM((2, rows) + tile, low),
            pltpu.VMEM((2, rows) + tile, low),
            dma((1,)),
            dma((1,)),
            dma((n_z,)),
            dma((1,)),
            dma((n_z,)),
            dma((n_z,)),
            dma((n_z,)),
            dma((1,)),
            dma((1,)),
            dma((1,)),
            dma((1,)),
            dma((1,)),
            pltpu.SemaphoreType.REGULAR((max(1, rounds - 1),)),
        ],
        compiler_params=pltpu.CompilerParams(
            collective_id=0, has_side_effects=True, vmem_limit_bytes=67043328 - out_bytes
        ),
    )(stride_owner.T, queries, keys, values, grad_out)
    out = jax.ShapeDtypeStruct((n_head, BLOCK, width), low)
    settled = pl.pallas_call(
        partial(settle_kernel, 4, n_head),
        out_shape=(out,) * 4,
        in_specs=[pl.BlockSpec(memory_space=pltpu.VMEM)],
        out_specs=(pl.BlockSpec(memory_space=pl.ANY),) * 4,
        scratch_shapes=[dma((4 * n_head,))],
        compiler_params=pltpu.CompilerParams(vmem_limit_bytes=8 << 20),
    )(arrived)
    return tuple(part.reshape(seq_rows, width) for part in settled)


def on_device(queries, keys, values, grad_out, stride_owner):
    n_head, n_blk = lax.axis_size("head"), lax.axis_size("blk")
    rows, width = queries.shape
    whole_heads = n_blk % 2 == 0 and width == n_head * (n_blk // 2) * HEAD_DIM
    if rows == BLOCK and whole_heads and n_head & (n_head - 1) == 0:
        return by_heads(queries, keys, values, grad_out, stride_owner)
    return by_runs(queries, keys, values, grad_out, stride_owner)


def solution(mesh):
    return jax.shard_map(
        on_device,
        mesh=mesh,
        in_specs=(
            P(("blk", "head"), None),
            P(("blk", "head"), None),
            P(("blk", "head"), None),
            P(("blk", "head"), None),
            P(),
        ),
        out_specs=(P("blk", "head"), P("blk", "head"), P("blk", "head"), P("blk", "head")),
        check_vma=False,
    )
```

```python
import math
from functools import partial

import jax
import jax.numpy as jnp
from jax import lax
from jax.experimental import pallas as pl
from jax.experimental.pallas import tpu as pltpu
from jax.sharding import PartitionSpec as P

HEAD_DIM = 128
BLOCK = 128
PICKS = 3
MESH = pl.DeviceIdType.MESH


def with_halo(block, sides, width):
    for axis, dim in sides:
        count = lax.axis_size(axis)
        forward = [(i, i + 1) for i in range(count - 1)]
        forward.append((count - 1, 0))
        backward = [(target, source) for source, target in forward]
        low = lax.ppermute(
            lax.slice_in_dim(block, block.shape[dim] - width, None, axis=dim), axis, forward
        )
        high = lax.ppermute(lax.slice_in_dim(block, 0, width, axis=dim), axis, backward)
        block = jnp.concatenate([low, block, high], axis=dim)
    return block


def from_root(block, axis, holder):
    block = jnp.where(lax.axis_index(axis) == holder, block, jnp.zeros_like(block))
    return lax.psum(block, axis)


def slot_tables(stride_owner, n_blk, blocks, capacity, device):
    owner_table = stride_owner.reshape(n_blk, blocks, PICKS)
    owner_ids = jnp.arange(n_blk, dtype=jnp.int32)
    naming = jnp.any(owner_table[:, :, :, None] == owner_ids[None, None, None, :], axis=2)
    counts = naming.astype(jnp.int32)
    ranking = jnp.cumsum(counts, axis=1) - counts
    naming_here = lax.dynamic_index_in_dim(naming, device, 2, keepdims=False)
    ranking_here = lax.dynamic_index_in_dim(ranking, device, 2, keepdims=False)
    slot_ids = jnp.arange(capacity, dtype=jnp.int32)
    matched = naming_here[:, None, :] & (ranking_here[:, None, :] == slot_ids[None, :, None])
    offsets = jnp.sum(
        matched.astype(jnp.int32) * jnp.arange(blocks, dtype=jnp.int32)[None, None, :], axis=2
    )
    own_rows = lax.dynamic_index_in_dim(owner_table, device, 0, keepdims=False)
    own_ranks = lax.dynamic_index_in_dim(ranking, device, 0, keepdims=False)
    picked = jnp.take_along_axis(own_ranks, own_rows, axis=1)
    flat_slot = own_rows * capacity + picked
    return (offsets.reshape(-1), flat_slot, matched.reshape(n_blk * capacity, blocks))


def fetch_keys(stacked, offsets, flat_slot, capacity):
    seq_rows = stacked.shape[1]
    width = stacked.shape[2]
    blocks = seq_rows // BLOCK
    n_blk = lax.axis_size("blk")
    extended = with_halo(stacked, (("blk", 1),), BLOCK)
    extended = extended.reshape(2, blocks + 2, BLOCK, width)
    block_view = stacked.reshape(2, blocks, BLOCK, width)
    leading = from_root(block_view[:, 0:2], "blk", 0)
    outgoing = jnp.take(block_view, offsets, axis=1).reshape(2, n_blk, capacity, BLOCK, width)
    incoming = lax.all_to_all(outgoing, "blk", split_axis=1, concat_axis=1, tiled=True)
    incoming = incoming.reshape(2, n_blk * capacity, BLOCK, width)
    pooled = jnp.concatenate([extended, incoming, leading], axis=1)
    rows_here = jnp.arange(blocks, dtype=jnp.int32)[:, None]
    nearby_index = rows_here + jnp.arange(3, dtype=jnp.int32)[None, :]
    distant_index = blocks + 2 + flat_slot
    leading_index = (
        jnp.zeros((blocks, 2), jnp.int32)
        + (blocks + 2 + n_blk * capacity)
        + jnp.arange(2, dtype=jnp.int32)[None, :]
    )
    table = jnp.concatenate([nearby_index, distant_index, leading_index], axis=1)
    return jnp.take(pooled, table.reshape(-1), axis=1)


def score_block(query_part, key_part, factor):
    return (
        jnp.einsum("gqhd,gjkhd->ghqjk", query_part, key_part, preferred_element_type=jnp.float32)
        * factor
    )


def log_normal(scores):
    row_max = jnp.max(scores, axis=(3, 4), keepdims=True)
    return row_max + jnp.log(jnp.sum(jnp.exp(scores - row_max), axis=(3, 4), keepdims=True))


def output_of(rounded, value_part):
    return jnp.einsum(
        "ghqjk,gjkhd->gqhd", rounded, value_part, preferred_element_type=jnp.float32
    ).astype(jnp.bfloat16)


def split_terms(coeffs, source):
    group_size = source.shape[0]
    near = jnp.einsum(
        "ghqjk,gqhd->gjkhd", coeffs[:, :, :, 0:3], source, preferred_element_type=jnp.float32
    )
    far = jnp.einsum(
        "ghqjk,gqhd->gjkhd", coeffs[:, :, :, 3:6], source, preferred_element_type=jnp.float32
    ).astype(jnp.bfloat16)
    lead = jnp.einsum(
        "ghqjk,gqhd->jkhd", coeffs[:, :, :, 6:8], source, preferred_element_type=jnp.float32
    )
    near = near.reshape(group_size, 3, near.shape[2], near.shape[3] * near.shape[4])
    far = far.reshape(group_size, 3, far.shape[2], far.shape[3] * far.shape[4])
    lead = lead.reshape(2, lead.shape[1], lead.shape[2] * lead.shape[3])
    return (near, far, lead)


def backward_from(
    scores, log_total, rounded, attended, grad_part, query_part, key_part, value_part, factor
):
    grad_weights = jnp.einsum(
        "gqhd,gjkhd->ghqjk", grad_part, value_part, preferred_element_type=jnp.float32
    )
    delta = jnp.sum(grad_part.astype(jnp.float32) * attended.astype(jnp.float32), axis=3)
    delta = jnp.transpose(delta, (0, 2, 1))[:, :, :, None, None]
    grad_scores = (jnp.exp(scores - log_total) * (grad_weights - delta) * factor).astype(
        jnp.bfloat16
    )
    grad_query = jnp.einsum(
        "ghqjk,gjkhd->gqhd", grad_scores, key_part, preferred_element_type=jnp.float32
    ).astype(jnp.bfloat16)
    key_near, key_far, key_lead = split_terms(grad_scores, query_part)
    value_near, value_far, value_lead = split_terms(rounded, grad_part)
    return (grad_query, key_near, key_far, key_lead, value_near, value_far, value_lead)


def spread_near(near_terms, width):
    blank = jnp.zeros((1, BLOCK, width), jnp.float32)
    return (
        jnp.concatenate([near_terms[:, 0], blank, blank], axis=0)
        + jnp.concatenate([blank, near_terms[:, 1], blank], axis=0)
        + jnp.concatenate([blank, blank, near_terms[:, 2]], axis=0)
    )


def by_runs(queries, keys, values, grad_out, stride_owner):
    query_rows, key_rows, value_rows, grad_rows = (
        lax.all_to_all(queries, "head", split_axis=1, concat_axis=0, tiled=True),
        lax.all_to_all(keys, "head", split_axis=1, concat_axis=0, tiled=True),
        lax.all_to_all(values, "head", split_axis=1, concat_axis=0, tiled=True),
        lax.all_to_all(grad_out, "head", split_axis=1, concat_axis=0, tiled=True),
    )
    seq_rows, width = query_rows.shape
    heads_here = width // HEAD_DIM
    blocks = seq_rows // BLOCK
    n_blk = lax.axis_size("blk")
    capacity = max(2, (PICKS * blocks + n_blk - 1) // n_blk)
    device = lax.axis_index("blk")
    offsets, flat_slot, matched = slot_tables(stride_owner, n_blk, blocks, capacity, device)
    group_size = math.gcd(blocks, max(1, 512 // BLOCK))
    group_count = blocks // group_size
    factor = HEAD_DIM ** (-0.5)
    stacked = jnp.stack([key_rows, value_rows])
    query_view = query_rows.reshape(blocks, BLOCK, heads_here, HEAD_DIM)
    grad_view = grad_rows.reshape(blocks, BLOCK, heads_here, HEAD_DIM)
    key_sets = fetch_keys(stacked, offsets, flat_slot, capacity)
    key_sets = key_sets.reshape(2, blocks, 8, BLOCK, heads_here, HEAD_DIM)

    def pieces(group_id):
        start = group_id * group_size
        query_part = lax.dynamic_slice_in_dim(query_view, start, group_size, 0)
        grad_part = lax.dynamic_slice_in_dim(grad_view, start, group_size, 0)
        kv_part = lax.dynamic_slice_in_dim(key_sets, start, group_size, 1)
        return (query_part, grad_part, kv_part[0], kv_part[1])

    def joined_pass(group_id):
        query_part, grad_part, key_part, value_part = pieces(group_id)
        scores = score_block(query_part, key_part, factor)
        log_total = log_normal(scores)
        rounded = jnp.exp(scores - log_total).astype(jnp.bfloat16)
        attended = output_of(rounded, value_part)
        extra = backward_from(
            scores,
            log_total,
            rounded,
            attended,
            grad_part,
            query_part,
            key_part,
            value_part,
            factor,
        )
        return (attended,) + extra

    group_ids = jnp.arange(group_count, dtype=jnp.int32)
    results = lax.map(joined_pass, group_ids)
    attended = results[0]
    grad_query, key_near, key_far, key_lead, value_near, value_far, value_lead = results[1:]
    key_ext = spread_near(key_near.reshape(blocks, 3, BLOCK, width), width)
    value_ext = spread_near(value_near.reshape(blocks, 3, BLOCK, width), width)
    rim_terms = jnp.stack(
        [
            jnp.stack([key_ext[0], value_ext[0]]),
            jnp.stack([key_ext[blocks + 1], value_ext[blocks + 1]]),
        ]
    )
    beside = with_halo(rim_terms.astype(jnp.bfloat16), (("blk", 0),), 1).astype(rim_terms.dtype)
    key_owned = key_ext[1 : blocks + 1].at[0].add(beside[0, 0]).at[blocks - 1].add(beside[3, 0])
    value_owned = value_ext[1 : blocks + 1].at[0].add(beside[0, 1]).at[blocks - 1].add(beside[3, 1])
    slot_flat = flat_slot.reshape(-1)
    key_back = (
        jnp.zeros((n_blk * capacity, BLOCK, width), jnp.bfloat16)
        .at[slot_flat]
        .set(key_far.reshape(blocks * PICKS, BLOCK, width))
    )
    value_back = (
        jnp.zeros((n_blk * capacity, BLOCK, width), jnp.bfloat16)
        .at[slot_flat]
        .set(value_far.reshape(blocks * PICKS, BLOCK, width))
    )
    key_arrived, value_arrived = (
        lax.all_to_all(
            key_back.reshape(n_blk, capacity, BLOCK, width),
            "blk",
            split_axis=0,
            concat_axis=0,
            tiled=True,
        ),
        lax.all_to_all(
            value_back.reshape(n_blk, capacity, BLOCK, width),
            "blk",
            split_axis=0,
            concat_axis=0,
            tiled=True,
        ),
    )
    match_b = matched.astype(jnp.bfloat16)
    key_owned = key_owned + jnp.einsum(
        "sr,sbc->rbc",
        match_b,
        key_arrived.reshape(n_blk * capacity, BLOCK, width),
        preferred_element_type=jnp.float32,
    )
    value_owned = value_owned + jnp.einsum(
        "sr,sbc->rbc",
        match_b,
        value_arrived.reshape(n_blk * capacity, BLOCK, width),
        preferred_element_type=jnp.float32,
    )
    key_total, value_total = (
        lax.psum(jnp.sum(key_lead, axis=0).astype(jnp.bfloat16), "blk").astype(jnp.float32),
        lax.psum(jnp.sum(value_lead, axis=0).astype(jnp.bfloat16), "blk").astype(jnp.float32),
    )
    at_root = device == 0
    key_owned = key_owned.at[0:2].add(jnp.where(at_root, key_total, jnp.zeros_like(key_total)))
    value_owned = value_owned.at[0:2].add(
        jnp.where(at_root, value_total, jnp.zeros_like(value_total))
    )
    grad_keys = key_owned.astype(jnp.bfloat16).reshape(seq_rows, width)
    grad_values = value_owned.astype(jnp.bfloat16).reshape(seq_rows, width)
    return (
        attended.reshape(seq_rows, width),
        grad_query.reshape(seq_rows, width),
        grad_keys,
        grad_values,
    )


def head_kernel(
    n_head,
    n_z,
    owner_in,
    q_in,
    k_in,
    v_in,
    g_in,
    out,
    owner_ref,
    kv_all,
    qg_all,
    k_sum,
    v_sum,
    k_far,
    v_far,
    stage,
    give,
    take,
    owner_sem,
    in_send,
    kv_recv,
    qg_recv,
    pass_send,
    pass_recv,
    pair_send,
    pair_recv,
    out_send,
    out_recv,
    near_sem,
):
    head = lax.axis_index("head")
    blk = lax.axis_index("blk")
    z = blk // 2
    c = blk % 2
    runs = n_head
    total_blocks = 2 * n_z * runs
    factor = HEAD_DIM ** (-0.5)
    my_head = head * n_z + z
    mine = blk * runs + head
    my_row = z * runs + head
    sibling = {"head": head, "blk": 2 * z + 1 - c}

    def columns(head_id):
        return pl.ds(pl.multiple_of(head_id * HEAD_DIM, HEAD_DIM), HEAD_DIM)

    bits = [1 << b for b in range(n_head.bit_length() - 1)]

    def greet(sem):
        for flip in bits:
            pl.semaphore_signal(
                sem,
                inc=1,
                device_id={"head": flipped(head, flip), "blk": blk},
                device_id_type=MESH,
            )
        pl.semaphore_signal(sem, inc=1, device_id=sibling, device_id_type=MESH)

        @pl.when(z > 0)
        def _():
            pl.semaphore_signal(
                sem, inc=1, device_id={"head": head, "blk": blk - 2}, device_id_type=MESH
            )

        @pl.when(z < n_z - 1)
        def _():
            pl.semaphore_signal(
                sem, inc=1, device_id={"head": head, "blk": blk + 2}, device_id_type=MESH
            )

    def flipped(head_id, flips):
        moved = head_id
        for flip in bits:
            if flips & flip:
                moved = moved + flip - 2 * flip * ((head_id // flip) % 2)
        return moved

    def hear(sem):
        ends = len(bits) + 1 + (z > 0).astype(jnp.int32) + (z < n_z - 1).astype(jnp.int32)
        pl.semaphore_wait(sem, ends)

    barrier = pltpu.get_barrier_semaphore()
    greet(barrier)

    local = [pltpu.make_async_copy(owner_in, owner_ref, owner_sem.at[0])]
    for at, source in enumerate((k_in, v_in)):
        local.append(
            pltpu.make_async_copy(
                source.at[:, columns(my_head)], kv_all.at[at, mine], kv_recv.at[0]
            )
        )
    for at, source in enumerate((q_in, g_in)):
        local.append(
            pltpu.make_async_copy(
                source.at[:, columns(my_head)], qg_all.at[at, my_row], qg_recv.at[0]
            )
        )
    for copy in local:
        copy.start()

    def push(at, source, target, slot, send_sem, recv_sem, z2, flips):
        h2 = flipped(head, flips)
        pltpu.make_async_remote_copy(
            src_ref=source.at[:, columns(h2 * n_z + z2)],
            dst_ref=target.at[at, slot],
            send_sem=send_sem.at[0],
            recv_sem=recv_sem,
            device_id={"head": h2, "blk": 2 * z2 + c},
            device_id_type=MESH,
        ).start()

    def push_pair(sources, target, slot, send_sem, recv_sem, dz, flips):
        for sign in (1, -1) if dz else (1,):
            z2 = z + sign * dz

            @pl.when((z2 >= 0) & (z2 < n_z))
            def _(z2=z2):
                arrive = recv_sem.at[(z2 + n_z - z) % n_z]
                for at, source in enumerate(sources):
                    push(at, source, target, slot, send_sem, arrive, z2, flips)

    def hops(flips):
        return sum(1 for flip in bits if flips & flip)

    everyone = sorted(
        (dz + hops(flips), -dz, flips)
        for dz in range(n_z)
        for flips in range(n_head)
        if dz + hops(flips) > 0
    )
    rounds = n_z - 1 + len(bits)
    for distance in range(1, rounds + 1):
        if distance == 1:
            hear(barrier)
        else:
            hear(near_sem.at[distance - 2])
        if distance < rounds:
            greet(near_sem.at[distance - 1])
        for hop, minus, flips in everyone:
            if hop == distance:
                push_pair((k_in, v_in), kv_all, mine, in_send, kv_recv, -minus, flips)
                if (-minus, flips) == (1, 0):
                    push_pair((q_in, g_in), qg_all, my_row, in_send, qg_recv, 1, 0)
    for dz in [n_z // 2] + [d for d in range(n_z - 1, -1, -1) if d != n_z // 2]:
        for flips in range(n_head):
            if dz + hops(flips) > 0 and (dz, flips) != (1, 0):
                push_pair((q_in, g_in), qg_all, my_row, in_send, qg_recv, dz, flips)

    blank = jnp.zeros((BLOCK, HEAD_DIM), jnp.float32)

    def clear(n, carry):
        k_sum[n] = blank
        v_sum[n] = blank
        return carry

    lax.fori_loop(0, total_blocks, clear, 0)
    none = n_z * runs * PICKS
    k_far[none] = blank.astype(jnp.bfloat16)
    v_far[none] = blank.astype(jnp.bfloat16)

    def await_bytes(ref, sem):
        pltpu.make_async_remote_copy(
            src_ref=ref,
            dst_ref=ref,
            send_sem=sem,
            recv_sem=sem,
            device_id=sibling,
            device_id_type=MESH,
        ).wait_recv()

    def run_of(dz, core):
        return 2 * ((z + n_z - dz) % n_z) + core

    order = [0, 1, n_z - 1] + list(range(2, n_z - 1))
    for dz in order[:n_z]:
        group = kv_all.at[:, pl.ds(run_of(dz, c) * runs, runs)]
        await_bytes(group, kv_recv.at[dz])
        pltpu.make_async_remote_copy(
            src_ref=group,
            dst_ref=group,
            send_sem=pass_send.at[0],
            recv_sem=pass_recv.at[0],
            device_id=sibling,
            device_id_type=MESH,
        ).start()
    local[0].wait()
    await_bytes(qg_all, pass_recv.at[0])

    def contract(left, right, dims):
        return lax.dot_general(
            left, right, ((dims[:1], dims[1:]), ((), ())), preferred_element_type=jnp.float32
        )

    def query_step(z1, r):
        row = z1 * runs + r
        block = (2 * z1 + c) * runs + r
        low = (block + total_blocks - 1) % total_blocks
        high = (block + 1) % total_blocks
        picks = [owner_ref[j, block] * runs + r for j in range(PICKS)]
        named = [low, block, high] + picks + [0, 1]
        keys = jnp.concatenate([kv_all[0, n] for n in named], axis=0)
        values = jnp.concatenate([kv_all[1, n] for n in named], axis=0)
        query = qg_all[0, row]
        grad = qg_all[1, row]
        scores = contract(keys, query, (1, 1))
        top = jnp.max(scores, axis=0, keepdims=True)
        weights = jnp.exp((scores - top) * factor)
        weights = weights * (1.0 / jnp.sum(weights, axis=0, keepdims=True))
        rounded = weights.astype(jnp.bfloat16)
        grad_weights = contract(values, grad, (1, 1))
        delta = jnp.sum(weights * grad_weights, axis=0, keepdims=True)
        grad_scores = (weights * (grad_weights - delta) * factor).astype(jnp.bfloat16)
        stage[0, row] = contract(rounded, values, (0, 0)).astype(jnp.bfloat16)
        stage[1, row] = contract(grad_scores, keys, (0, 0)).astype(jnp.bfloat16)
        key_terms = contract(grad_scores, query, (1, 0))
        value_terms = contract(rounded, grad, (1, 0))
        for j, n in ((0, low), (1, block), (2, high), (6, 0), (7, 1)):
            k_sum[n] += key_terms[j * BLOCK : (j + 1) * BLOCK]
            v_sum[n] += value_terms[j * BLOCK : (j + 1) * BLOCK]
        for j in range(PICKS):
            rows = slice((3 + j) * BLOCK, (4 + j) * BLOCK)
            k_far[row * PICKS + j] = key_terms[rows].astype(jnp.bfloat16)
            v_far[row * PICKS + j] = value_terms[rows].astype(jnp.bfloat16)

    def hand_out(first, dz):
        z2 = (z + n_z - dz) % n_z
        source = stage.at[pl.ds(first, 2), pl.ds(z2 * runs, runs)]
        target = out.at[pl.ds(first, 2), :, :, columns(z)]
        if dz == 0:
            pltpu.make_async_copy(source, target, out_recv.at[0]).start()
        else:
            pltpu.make_async_remote_copy(
                src_ref=source,
                dst_ref=target,
                send_sem=out_send.at[0],
                recv_sem=out_recv.at[0],
                device_id={"head": head, "blk": 2 * z2 + c},
                device_id_type=MESH,
            ).start()

    far_first = [dz for dz in (2, 1, 3, 0) if dz < n_z] + list(range(4, n_z))
    for dz in far_first:
        z1 = (z + n_z - dz) % n_z
        await_bytes(qg_all.at[:, pl.ds(z1 * runs, runs)], qg_recv.at[dz])

        def step(r, carry, z1=z1):
            query_step(z1, r)
            return carry

        lax.fori_loop(0, runs, step, 0)
        hand_out(0, dz)

    def total_of(sums, far, run, r):
        total = sums[run * runs + r]
        for z1 in range(n_z):
            block = (2 * z1 + c) * runs + r
            row = z1 * runs + r
            place = none
            for j in range(PICKS):
                place = jnp.where(owner_ref[j, block] == run, row * PICKS + j, place)
            total = total + far[place].astype(jnp.float32)
        return total

    def give_step(row, carry):
        run, r = 2 * (row // runs) + 1 - c, row % runs
        give[0, row] = total_of(k_sum, k_far, run, r).astype(jnp.bfloat16)
        give[1, row] = total_of(v_sum, v_far, run, r).astype(jnp.bfloat16)
        return carry

    lax.fori_loop(0, n_z * runs, give_step, 0)
    pair = pltpu.make_async_remote_copy(
        src_ref=give,
        dst_ref=take,
        send_sem=pair_send.at[0],
        recv_sem=pair_recv.at[0],
        device_id=sibling,
        device_id_type=MESH,
    )
    pair.start()
    pair.wait_recv()
    for dz in far_first:
        z1 = (z + n_z - dz) % n_z

        def join_step(r, carry, z1=z1):
            row, run = z1 * runs + r, 2 * z1 + c
            for at, sums, far in ((0, k_sum, k_far), (1, v_sum, v_far)):
                total = total_of(sums, far, run, r) + take[at, row].astype(jnp.float32)
                stage[2 + at, row] = total.astype(jnp.bfloat16)
            return carry

        lax.fori_loop(0, runs, join_step, 0)
        hand_out(2, dz)

    def await_sent(ref, sem):
        pltpu.make_async_remote_copy(
            src_ref=ref,
            dst_ref=ref,
            send_sem=sem,
            recv_sem=sem,
            device_id=sibling,
            device_id_type=MESH,
        ).wait_send()

    rows = n_z * runs
    pair.wait_send()
    await_sent(qg_all, pass_send.at[0])
    await_sent(kv_all.at[:, pl.ds(0, 2 * (rows - 1))], in_send.at[0])
    if n_z > 1:
        await_sent(kv_all.at[:, pl.ds(0, 2 * (rows - runs))], out_send.at[0])
    await_bytes(out, out_recv.at[0])


def settle_kernel(count, pieces, source, *refs):
    targets, sem = refs[:count], refs[count]
    copies = [
        pltpu.make_async_copy(
            source.at[at, piece], targets[at].at[piece], sem.at[0]
        )
        for at in range(count)
        for piece in range(pieces)
    ]
    for copy in copies:
        copy.start()
    pltpu.make_async_copy(source, source, sem.at[0]).wait()


def by_heads(queries, keys, values, grad_out, stride_owner):
    n_head, n_blk = lax.axis_size("head"), lax.axis_size("blk")
    n_z = n_blk // 2
    rows = n_z * n_head
    rounds = n_z - 1 + n_head.bit_length() - 1
    seq_rows, width = BLOCK * n_head, n_z * HEAD_DIM
    tile = (BLOCK, HEAD_DIM)
    low, wide = jnp.bfloat16, jnp.float32
    dma = pltpu.SemaphoreType.DMA
    out_bytes = 8 * seq_rows * width
    arrived = pl.pallas_call(
        partial(head_kernel, n_head, n_z),
        out_shape=pltpu.VMEM((4, n_head, BLOCK, width), low),
        in_specs=[pl.BlockSpec(memory_space=pltpu.HBM)] * 5,
        out_specs=pl.BlockSpec(memory_space=pltpu.VMEM),
        scratch_shapes=[
            pltpu.SMEM(stride_owner.shape[::-1], jnp.int32),
            pltpu.VMEM((2, 2 * rows) + tile, low),
            pltpu.VMEM((2, rows) + tile, low),
            pltpu.VMEM((2 * rows,) + tile, wide),
            pltpu.VMEM((2 * rows,) + tile, wide),
            pltpu.VMEM((rows * PICKS + 1,) + tile, low),
            pltpu.VMEM((rows * PICKS + 1,) + tile, low),
            pltpu.VMEM((4, rows) + tile, low),
            pltpu.VMEM((2, rows) + tile, low),
            pltpu.VMEM((2, rows) + tile, low),
            dma((1,)),
            dma((1,)),
            dma((n_z,)),
            dma((n_z,)),
            dma((1,)),
            dma((1,)),
            dma((1,)),
            dma((1,)),
            dma((1,)),
            dma((1,)),
            pltpu.SemaphoreType.REGULAR((max(1, rounds - 1),)),
        ],
        compiler_params=pltpu.CompilerParams(
            collective_id=0, has_side_effects=True, vmem_limit_bytes=67043328 - out_bytes
        ),
    )(stride_owner.T, queries, keys, values, grad_out)
    out = jax.ShapeDtypeStruct((n_head, BLOCK, width), low)
    settled = pl.pallas_call(
        partial(settle_kernel, 4, n_head),
        out_shape=(out,) * 4,
        in_specs=[pl.BlockSpec(memory_space=pltpu.VMEM)],
        out_specs=(pl.BlockSpec(memory_space=pl.ANY),) * 4,
        scratch_shapes=[dma((1,))],
        compiler_params=pltpu.CompilerParams(vmem_limit_bytes=8 << 20),
    )(arrived)
    return tuple(part.reshape(seq_rows, width) for part in settled)


def on_device(queries, keys, values, grad_out, stride_owner):
    n_head, n_blk = lax.axis_size("head"), lax.axis_size("blk")
    rows, width = queries.shape
    whole_heads = n_blk % 2 == 0 and width == n_head * (n_blk // 2) * HEAD_DIM
    if rows == BLOCK and whole_heads and n_head & (n_head - 1) == 0:
        return by_heads(queries, keys, values, grad_out, stride_owner)
    return by_runs(queries, keys, values, grad_out, stride_owner)


def solution(mesh):
    return jax.shard_map(
        on_device,
        mesh=mesh,
        in_specs=(
            P(("blk", "head"), None),
            P(("blk", "head"), None),
            P(("blk", "head"), None),
            P(("blk", "head"), None),
            P(),
        ),
        out_specs=(P("blk", "head"), P("blk", "head"), P("blk", "head"), P("blk", "head")),
        check_vma=False,
    )
```

```python
import math
from functools import partial

import jax
import jax.numpy as jnp
from jax import lax
from jax.experimental import pallas as pl
from jax.experimental.pallas import tpu as pltpu
from jax.sharding import PartitionSpec as P

HEAD_DIM = 128
BLOCK = 128
PICKS = 3
MESH = pl.DeviceIdType.MESH


def with_halo(block, sides, width):
    for axis, dim in sides:
        count = lax.axis_size(axis)
        forward = [(i, i + 1) for i in range(count - 1)]
        forward.append((count - 1, 0))
        backward = [(target, source) for source, target in forward]
        low = lax.ppermute(
            lax.slice_in_dim(block, block.shape[dim] - width, None, axis=dim), axis, forward
        )
        high = lax.ppermute(lax.slice_in_dim(block, 0, width, axis=dim), axis, backward)
        block = jnp.concatenate([low, block, high], axis=dim)
    return block


def from_root(block, axis, holder):
    block = jnp.where(lax.axis_index(axis) == holder, block, jnp.zeros_like(block))
    return lax.psum(block, axis)


def slot_tables(stride_owner, n_blk, blocks, capacity, device):
    owner_table = stride_owner.reshape(n_blk, blocks, PICKS)
    owner_ids = jnp.arange(n_blk, dtype=jnp.int32)
    naming = jnp.any(owner_table[:, :, :, None] == owner_ids[None, None, None, :], axis=2)
    counts = naming.astype(jnp.int32)
    ranking = jnp.cumsum(counts, axis=1) - counts
    naming_here = lax.dynamic_index_in_dim(naming, device, 2, keepdims=False)
    ranking_here = lax.dynamic_index_in_dim(ranking, device, 2, keepdims=False)
    slot_ids = jnp.arange(capacity, dtype=jnp.int32)
    matched = naming_here[:, None, :] & (ranking_here[:, None, :] == slot_ids[None, :, None])
    offsets = jnp.sum(
        matched.astype(jnp.int32) * jnp.arange(blocks, dtype=jnp.int32)[None, None, :], axis=2
    )
    own_rows = lax.dynamic_index_in_dim(owner_table, device, 0, keepdims=False)
    own_ranks = lax.dynamic_index_in_dim(ranking, device, 0, keepdims=False)
    picked = jnp.take_along_axis(own_ranks, own_rows, axis=1)
    flat_slot = own_rows * capacity + picked
    return (offsets.reshape(-1), flat_slot, matched.reshape(n_blk * capacity, blocks))


def fetch_keys(stacked, offsets, flat_slot, capacity):
    seq_rows = stacked.shape[1]
    width = stacked.shape[2]
    blocks = seq_rows // BLOCK
    n_blk = lax.axis_size("blk")
    extended = with_halo(stacked, (("blk", 1),), BLOCK)
    extended = extended.reshape(2, blocks + 2, BLOCK, width)
    block_view = stacked.reshape(2, blocks, BLOCK, width)
    leading = from_root(block_view[:, 0:2], "blk", 0)
    outgoing = jnp.take(block_view, offsets, axis=1).reshape(2, n_blk, capacity, BLOCK, width)
    incoming = lax.all_to_all(outgoing, "blk", split_axis=1, concat_axis=1, tiled=True)
    incoming = incoming.reshape(2, n_blk * capacity, BLOCK, width)
    pooled = jnp.concatenate([extended, incoming, leading], axis=1)
    rows_here = jnp.arange(blocks, dtype=jnp.int32)[:, None]
    nearby_index = rows_here + jnp.arange(3, dtype=jnp.int32)[None, :]
    distant_index = blocks + 2 + flat_slot
    leading_index = (
        jnp.zeros((blocks, 2), jnp.int32)
        + (blocks + 2 + n_blk * capacity)
        + jnp.arange(2, dtype=jnp.int32)[None, :]
    )
    table = jnp.concatenate([nearby_index, distant_index, leading_index], axis=1)
    return jnp.take(pooled, table.reshape(-1), axis=1)


def score_block(query_part, key_part, factor):
    return (
        jnp.einsum("gqhd,gjkhd->ghqjk", query_part, key_part, preferred_element_type=jnp.float32)
        * factor
    )


def log_normal(scores):
    row_max = jnp.max(scores, axis=(3, 4), keepdims=True)
    return row_max + jnp.log(jnp.sum(jnp.exp(scores - row_max), axis=(3, 4), keepdims=True))


def output_of(rounded, value_part):
    return jnp.einsum(
        "ghqjk,gjkhd->gqhd", rounded, value_part, preferred_element_type=jnp.float32
    ).astype(jnp.bfloat16)


def split_terms(coeffs, source):
    group_size = source.shape[0]
    near = jnp.einsum(
        "ghqjk,gqhd->gjkhd", coeffs[:, :, :, 0:3], source, preferred_element_type=jnp.float32
    )
    far = jnp.einsum(
        "ghqjk,gqhd->gjkhd", coeffs[:, :, :, 3:6], source, preferred_element_type=jnp.float32
    ).astype(jnp.bfloat16)
    lead = jnp.einsum(
        "ghqjk,gqhd->jkhd", coeffs[:, :, :, 6:8], source, preferred_element_type=jnp.float32
    )
    near = near.reshape(group_size, 3, near.shape[2], near.shape[3] * near.shape[4])
    far = far.reshape(group_size, 3, far.shape[2], far.shape[3] * far.shape[4])
    lead = lead.reshape(2, lead.shape[1], lead.shape[2] * lead.shape[3])
    return (near, far, lead)


def backward_from(
    scores, log_total, rounded, attended, grad_part, query_part, key_part, value_part, factor
):
    grad_weights = jnp.einsum(
        "gqhd,gjkhd->ghqjk", grad_part, value_part, preferred_element_type=jnp.float32
    )
    delta = jnp.sum(grad_part.astype(jnp.float32) * attended.astype(jnp.float32), axis=3)
    delta = jnp.transpose(delta, (0, 2, 1))[:, :, :, None, None]
    grad_scores = (jnp.exp(scores - log_total) * (grad_weights - delta) * factor).astype(
        jnp.bfloat16
    )
    grad_query = jnp.einsum(
        "ghqjk,gjkhd->gqhd", grad_scores, key_part, preferred_element_type=jnp.float32
    ).astype(jnp.bfloat16)
    key_near, key_far, key_lead = split_terms(grad_scores, query_part)
    value_near, value_far, value_lead = split_terms(rounded, grad_part)
    return (grad_query, key_near, key_far, key_lead, value_near, value_far, value_lead)


def spread_near(near_terms, width):
    blank = jnp.zeros((1, BLOCK, width), jnp.float32)
    return (
        jnp.concatenate([near_terms[:, 0], blank, blank], axis=0)
        + jnp.concatenate([blank, near_terms[:, 1], blank], axis=0)
        + jnp.concatenate([blank, blank, near_terms[:, 2]], axis=0)
    )


def by_runs(queries, keys, values, grad_out, stride_owner):
    query_rows, key_rows, value_rows, grad_rows = (
        lax.all_to_all(queries, "head", split_axis=1, concat_axis=0, tiled=True),
        lax.all_to_all(keys, "head", split_axis=1, concat_axis=0, tiled=True),
        lax.all_to_all(values, "head", split_axis=1, concat_axis=0, tiled=True),
        lax.all_to_all(grad_out, "head", split_axis=1, concat_axis=0, tiled=True),
    )
    seq_rows, width = query_rows.shape
    heads_here = width // HEAD_DIM
    blocks = seq_rows // BLOCK
    n_blk = lax.axis_size("blk")
    capacity = max(2, (PICKS * blocks + n_blk - 1) // n_blk)
    device = lax.axis_index("blk")
    offsets, flat_slot, matched = slot_tables(stride_owner, n_blk, blocks, capacity, device)
    group_size = math.gcd(blocks, max(1, 512 // BLOCK))
    group_count = blocks // group_size
    factor = HEAD_DIM ** (-0.5)
    stacked = jnp.stack([key_rows, value_rows])
    query_view = query_rows.reshape(blocks, BLOCK, heads_here, HEAD_DIM)
    grad_view = grad_rows.reshape(blocks, BLOCK, heads_here, HEAD_DIM)
    key_sets = fetch_keys(stacked, offsets, flat_slot, capacity)
    key_sets = key_sets.reshape(2, blocks, 8, BLOCK, heads_here, HEAD_DIM)

    def pieces(group_id):
        start = group_id * group_size
        query_part = lax.dynamic_slice_in_dim(query_view, start, group_size, 0)
        grad_part = lax.dynamic_slice_in_dim(grad_view, start, group_size, 0)
        kv_part = lax.dynamic_slice_in_dim(key_sets, start, group_size, 1)
        return (query_part, grad_part, kv_part[0], kv_part[1])

    def joined_pass(group_id):
        query_part, grad_part, key_part, value_part = pieces(group_id)
        scores = score_block(query_part, key_part, factor)
        log_total = log_normal(scores)
        rounded = jnp.exp(scores - log_total).astype(jnp.bfloat16)
        attended = output_of(rounded, value_part)
        extra = backward_from(
            scores,
            log_total,
            rounded,
            attended,
            grad_part,
            query_part,
            key_part,
            value_part,
            factor,
        )
        return (attended,) + extra

    group_ids = jnp.arange(group_count, dtype=jnp.int32)
    results = lax.map(joined_pass, group_ids)
    attended = results[0]
    grad_query, key_near, key_far, key_lead, value_near, value_far, value_lead = results[1:]
    key_ext = spread_near(key_near.reshape(blocks, 3, BLOCK, width), width)
    value_ext = spread_near(value_near.reshape(blocks, 3, BLOCK, width), width)
    rim_terms = jnp.stack(
        [
            jnp.stack([key_ext[0], value_ext[0]]),
            jnp.stack([key_ext[blocks + 1], value_ext[blocks + 1]]),
        ]
    )
    beside = with_halo(rim_terms.astype(jnp.bfloat16), (("blk", 0),), 1).astype(rim_terms.dtype)
    key_owned = key_ext[1 : blocks + 1].at[0].add(beside[0, 0]).at[blocks - 1].add(beside[3, 0])
    value_owned = value_ext[1 : blocks + 1].at[0].add(beside[0, 1]).at[blocks - 1].add(beside[3, 1])
    slot_flat = flat_slot.reshape(-1)
    key_back = (
        jnp.zeros((n_blk * capacity, BLOCK, width), jnp.bfloat16)
        .at[slot_flat]
        .set(key_far.reshape(blocks * PICKS, BLOCK, width))
    )
    value_back = (
        jnp.zeros((n_blk * capacity, BLOCK, width), jnp.bfloat16)
        .at[slot_flat]
        .set(value_far.reshape(blocks * PICKS, BLOCK, width))
    )
    key_arrived, value_arrived = (
        lax.all_to_all(
            key_back.reshape(n_blk, capacity, BLOCK, width),
            "blk",
            split_axis=0,
            concat_axis=0,
            tiled=True,
        ),
        lax.all_to_all(
            value_back.reshape(n_blk, capacity, BLOCK, width),
            "blk",
            split_axis=0,
            concat_axis=0,
            tiled=True,
        ),
    )
    match_b = matched.astype(jnp.bfloat16)
    key_owned = key_owned + jnp.einsum(
        "sr,sbc->rbc",
        match_b,
        key_arrived.reshape(n_blk * capacity, BLOCK, width),
        preferred_element_type=jnp.float32,
    )
    value_owned = value_owned + jnp.einsum(
        "sr,sbc->rbc",
        match_b,
        value_arrived.reshape(n_blk * capacity, BLOCK, width),
        preferred_element_type=jnp.float32,
    )
    key_total, value_total = (
        lax.psum(jnp.sum(key_lead, axis=0).astype(jnp.bfloat16), "blk").astype(jnp.float32),
        lax.psum(jnp.sum(value_lead, axis=0).astype(jnp.bfloat16), "blk").astype(jnp.float32),
    )
    at_root = device == 0
    key_owned = key_owned.at[0:2].add(jnp.where(at_root, key_total, jnp.zeros_like(key_total)))
    value_owned = value_owned.at[0:2].add(
        jnp.where(at_root, value_total, jnp.zeros_like(value_total))
    )
    grad_keys = key_owned.astype(jnp.bfloat16).reshape(seq_rows, width)
    grad_values = value_owned.astype(jnp.bfloat16).reshape(seq_rows, width)
    return (
        attended.reshape(seq_rows, width),
        grad_query.reshape(seq_rows, width),
        grad_keys,
        grad_values,
    )


def head_bits(n_head):
    return [1 << bit for bit in range(n_head.bit_length() - 1)]


def neighbours(n_head, n_z, at_z):
    beside = [(at_z, flip, 0) for flip in head_bits(n_head)] + [(at_z, 0, 1)]
    return beside + [(z2, 0, 0) for z2 in (at_z - 1, at_z + 1) if 0 <= z2 < n_z]


def seen_from(peer, at_z):
    return (at_z, peer[1], peer[2])


def entry_rounds(n_head, n_z):
    middle = n_z // 2
    hears, knows = [], []
    near = [neighbours(n_head, n_z, at_z) for at_z in range(n_z)]
    first = [set(near[at_z]) for at_z in range(n_z)]
    if middle:
        first[middle] = {(middle - 1, 0, 0)}
    hears.append(first)
    knows.append([{(at_z, 0, 0)} | first[at_z] for at_z in range(n_z)])
    reached = [
        {(z2, flips, 0) for z2 in range(n_z) for flips in range(n_head)} | {(at_z, 0, 1)}
        for at_z in range(n_z)
    ]
    while any(want - known for want, known in zip(reached, knows[-1])):
        known = knows[-1]
        heard = [
            {p for p in near[at_z] if seen_from(p, at_z) in known[p[0]]} for at_z in range(n_z)
        ]
        hears.append(heard)
        knows.append(
            [
                known[at_z].union(
                    *(
                        {(k[0], k[1] ^ p[1], k[2] ^ p[2]) for k in known[p[0]]}
                        for p in heard[at_z]
                    )
                )
                for at_z in range(n_z)
            ]
        )
    return hears, knows


def head_kernel(
    n_head,
    n_z,
    owner_in,
    q_in,
    k_in,
    v_in,
    g_in,
    out,
    owner_ref,
    kv_all,
    qg_all,
    k_sum,
    v_sum,
    k_far,
    v_far,
    stage,
    give,
    take,
    owner_sem,
    in_send,
    kv_recv,
    qg_recv,
    pass_send,
    pass_recv,
    pair_send,
    pair_recv,
    out_send,
    out_recv,
    near_sem,
):
    head = lax.axis_index("head")
    blk = lax.axis_index("blk")
    z = blk // 2
    c = blk % 2
    runs = n_head
    total_blocks = 2 * n_z * runs
    factor = HEAD_DIM ** (-0.5)
    my_head = head * n_z + z
    mine = blk * runs + head
    my_row = z * runs + head
    sibling = {"head": head, "blk": 2 * z + 1 - c}

    def columns(head_id):
        return pl.ds(pl.multiple_of(head_id * HEAD_DIM, HEAD_DIM), HEAD_DIM)

    bits = head_bits(n_head)
    hears, knows = entry_rounds(n_head, n_z)
    barrier = pltpu.get_barrier_semaphore()

    def flipped(flips):
        moved = head
        for flip in bits:
            if flips & flip:
                moved = moved + flip - 2 * flip * ((head // flip) % 2)
        return moved

    def place(peer):
        at_z, flips, other = peer
        return {"head": flipped(flips), "blk": 2 * at_z + (1 - c if other else c)}

    def greet(at_z, step):
        sem = barrier if step == 0 else near_sem.at[step - 1]
        for peer in neighbours(n_head, n_z, at_z):
            if seen_from(peer, at_z) in hears[step][peer[0]]:
                pl.semaphore_signal(sem, inc=1, device_id=place(peer), device_id_type=MESH)

    def hear(at_z, step):
        sem = barrier if step == 0 else near_sem.at[step - 1]
        if hears[step][at_z]:
            pl.semaphore_wait(sem, len(hears[step][at_z]))

    def push(sources, target, slot, recv_sem, at_z, peer):
        z2, flips, _ = peer
        for at, source in enumerate(sources):
            pltpu.make_async_remote_copy(
                src_ref=source.at[:, columns(flipped(flips) * n_z + z2)],
                dst_ref=target.at[at, slot],
                send_sem=in_send.at[0],
                recv_sem=recv_sem.at[(z2 + n_z - at_z) % n_z],
                device_id=place(peer),
                device_id_type=MESH,
            ).start()

    def crosses(at_z, peer):
        return (at_z < n_z // 2) != (peer[0] < n_z // 2)

    def urgency(at_z, peer):
        hops = abs(peer[0] - at_z) + bin(peer[1]).count("1")
        return (not crosses(at_z, peer), hops, peer)

    def enter(at_z):
        greet(at_z, 0)
        local = [pltpu.make_async_copy(owner_in, owner_ref, owner_sem.at[0])]
        for sources, target, slot, sem in (
            ((k_in, v_in), kv_all, mine, kv_recv),
            ((q_in, g_in), qg_all, my_row, qg_recv),
        ):
            for at, source in enumerate(sources):
                local.append(
                    pltpu.make_async_copy(
                        source.at[:, columns(my_head)], target.at[at, slot], sem.at[0]
                    )
                )
        for copy in local:
            copy.start()
        early = []
        met = {(at_z, 0, 0)}
        for step in range(len(hears)):
            hear(at_z, step)
            fresh = [p for p in knows[step][at_z] - met if not p[2]]
            met |= knows[step][at_z]
            fresh.sort(key=partial(urgency, at_z))
            first = [p for p in fresh if step == 0 and crosses(at_z, p)]
            for peer in first:
                push((k_in, v_in), kv_all, mine, kv_recv, at_z, peer)
                push((q_in, g_in), qg_all, my_row, qg_recv, at_z, peer)
            early += first
            if step + 1 < len(hears):
                greet(at_z, step + 1)
            for peer in fresh:
                if peer not in first:
                    push((k_in, v_in), kv_all, mine, kv_recv, at_z, peer)
        late = [p for p in met if not p[2] and p[:2] != (at_z, 0) and p not in early]
        for dz in [n_z // 2] + [d for d in range(n_z - 1, -1, -1) if d != n_z // 2]:
            for peer in sorted(late, key=partial(urgency, at_z)):
                if abs(peer[0] - at_z) == dz:
                    push((q_in, g_in), qg_all, my_row, qg_recv, at_z, peer)

    for at_z in range(n_z):
        pl.when(z == at_z)(partial(enter, at_z))

    blank = jnp.zeros((BLOCK, HEAD_DIM), jnp.float32)

    def clear(n, carry):
        k_sum[n] = blank
        v_sum[n] = blank
        return carry

    lax.fori_loop(0, total_blocks, clear, 0)
    none = n_z * runs * PICKS
    k_far[none] = blank.astype(jnp.bfloat16)
    v_far[none] = blank.astype(jnp.bfloat16)

    def await_bytes(ref, sem):
        pltpu.make_async_remote_copy(
            src_ref=ref,
            dst_ref=ref,
            send_sem=sem,
            recv_sem=sem,
            device_id=sibling,
            device_id_type=MESH,
        ).wait_recv()

    def run_of(dz, core):
        return 2 * ((z + n_z - dz) % n_z) + core

    order = [0, 1, n_z - 1] + list(range(2, n_z - 1))
    for dz in order[:n_z]:
        group = kv_all.at[:, pl.ds(run_of(dz, c) * runs, runs)]
        await_bytes(group, kv_recv.at[dz])
        pltpu.make_async_remote_copy(
            src_ref=group,
            dst_ref=group,
            send_sem=pass_send.at[0],
            recv_sem=pass_recv.at[0],
            device_id=sibling,
            device_id_type=MESH,
        ).start()
    pltpu.make_async_copy(owner_in, owner_ref, owner_sem.at[0]).wait()
    await_bytes(qg_all, pass_recv.at[0])

    def contract(left, right, dims):
        return lax.dot_general(
            left, right, ((dims[:1], dims[1:]), ((), ())), preferred_element_type=jnp.float32
        )

    def query_step(z1, r):
        row = z1 * runs + r
        block = (2 * z1 + c) * runs + r
        low = (block + total_blocks - 1) % total_blocks
        high = (block + 1) % total_blocks
        picks = [owner_ref[j, block] * runs + r for j in range(PICKS)]
        named = [low, block, high] + picks + [0, 1]
        keys = jnp.concatenate([kv_all[0, n] for n in named], axis=0)
        values = jnp.concatenate([kv_all[1, n] for n in named], axis=0)
        query = qg_all[0, row]
        grad = qg_all[1, row]
        scores = contract(keys, query, (1, 1))
        top = jnp.max(scores, axis=0, keepdims=True)
        weights = jnp.exp((scores - top) * factor)
        weights = weights * (1.0 / jnp.sum(weights, axis=0, keepdims=True))
        rounded = weights.astype(jnp.bfloat16)
        grad_weights = contract(values, grad, (1, 1))
        delta = jnp.sum(weights * grad_weights, axis=0, keepdims=True)
        grad_scores = (weights * (grad_weights - delta) * factor).astype(jnp.bfloat16)
        stage[0, row] = contract(rounded, values, (0, 0)).astype(jnp.bfloat16)
        stage[1, row] = contract(grad_scores, keys, (0, 0)).astype(jnp.bfloat16)
        key_terms = contract(grad_scores, query, (1, 0))
        value_terms = contract(rounded, grad, (1, 0))
        for j, n in ((0, low), (1, block), (2, high), (6, 0), (7, 1)):
            k_sum[n] += key_terms[j * BLOCK : (j + 1) * BLOCK]
            v_sum[n] += value_terms[j * BLOCK : (j + 1) * BLOCK]
        for j in range(PICKS):
            rows = slice((3 + j) * BLOCK, (4 + j) * BLOCK)
            k_far[row * PICKS + j] = key_terms[rows].astype(jnp.bfloat16)
            v_far[row * PICKS + j] = value_terms[rows].astype(jnp.bfloat16)

    def hand_out(first, dz):
        z2 = (z + n_z - dz) % n_z
        source = stage.at[pl.ds(first, 2), pl.ds(z2 * runs, runs)]
        target = out.at[pl.ds(first, 2), :, :, columns(z)]
        if dz == 0:
            pltpu.make_async_copy(source, target, out_recv.at[0]).start()
        else:
            pltpu.make_async_remote_copy(
                src_ref=source,
                dst_ref=target,
                send_sem=out_send.at[0],
                recv_sem=out_recv.at[0],
                device_id={"head": head, "blk": 2 * z2 + c},
                device_id_type=MESH,
            ).start()

    far_first = [dz for dz in (2, 1, 3, 0) if dz < n_z] + list(range(4, n_z))
    for dz in far_first:
        z1 = (z + n_z - dz) % n_z
        await_bytes(qg_all.at[:, pl.ds(z1 * runs, runs)], qg_recv.at[dz])

        def step(r, carry, z1=z1):
            query_step(z1, r)
            return carry

        lax.fori_loop(0, runs, step, 0)
        hand_out(0, dz)

    def total_of(sums, far, run, r):
        total = sums[run * runs + r]
        for z1 in range(n_z):
            block = (2 * z1 + c) * runs + r
            row = z1 * runs + r
            place = none
            for j in range(PICKS):
                place = jnp.where(owner_ref[j, block] == run, row * PICKS + j, place)
            total = total + far[place].astype(jnp.float32)
        return total

    def give_step(row, carry):
        run, r = 2 * (row // runs) + 1 - c, row % runs
        give[0, row] = total_of(k_sum, k_far, run, r).astype(jnp.bfloat16)
        give[1, row] = total_of(v_sum, v_far, run, r).astype(jnp.bfloat16)
        return carry

    lax.fori_loop(0, n_z * runs, give_step, 0)
    pair = pltpu.make_async_remote_copy(
        src_ref=give,
        dst_ref=take,
        send_sem=pair_send.at[0],
        recv_sem=pair_recv.at[0],
        device_id=sibling,
        device_id_type=MESH,
    )
    pair.start()
    pair.wait_recv()
    for dz in far_first:
        z1 = (z + n_z - dz) % n_z

        def join_step(r, carry, z1=z1):
            row, run = z1 * runs + r, 2 * z1 + c
            for at, sums, far in ((0, k_sum, k_far), (1, v_sum, v_far)):
                total = total_of(sums, far, run, r) + take[at, row].astype(jnp.float32)
                stage[2 + at, row] = total.astype(jnp.bfloat16)
            return carry

        lax.fori_loop(0, runs, join_step, 0)
        hand_out(2, dz)

    def await_sent(ref, sem):
        pltpu.make_async_remote_copy(
            src_ref=ref,
            dst_ref=ref,
            send_sem=sem,
            recv_sem=sem,
            device_id=sibling,
            device_id_type=MESH,
        ).wait_send()

    rows = n_z * runs
    pair.wait_send()
    await_sent(qg_all, pass_send.at[0])
    await_sent(kv_all.at[:, pl.ds(0, 2 * (rows - 1))], in_send.at[0])
    if n_z > 1:
        await_sent(kv_all.at[:, pl.ds(0, 2 * (rows - runs))], out_send.at[0])
    await_bytes(out, out_recv.at[0])


def settle_kernel(count, pieces, source, *refs):
    targets, sem = refs[:count], refs[count]
    copies = [
        pltpu.make_async_copy(
            source.at[at, piece], targets[at].at[piece], sem.at[0]
        )
        for at in range(count)
        for piece in range(pieces)
    ]
    for copy in copies:
        copy.start()
    pltpu.make_async_copy(source, source, sem.at[0]).wait()


def by_heads(queries, keys, values, grad_out, stride_owner):
    n_head, n_blk = lax.axis_size("head"), lax.axis_size("blk")
    n_z = n_blk // 2
    rows = n_z * n_head
    rounds = len(entry_rounds(n_head, n_z)[0])
    seq_rows, width = BLOCK * n_head, n_z * HEAD_DIM
    tile = (BLOCK, HEAD_DIM)
    low, wide = jnp.bfloat16, jnp.float32
    dma = pltpu.SemaphoreType.DMA
    out_bytes = 8 * seq_rows * width
    arrived = pl.pallas_call(
        partial(head_kernel, n_head, n_z),
        out_shape=pltpu.VMEM((4, n_head, BLOCK, width), low),
        in_specs=[pl.BlockSpec(memory_space=pltpu.HBM)] * 5,
        out_specs=pl.BlockSpec(memory_space=pltpu.VMEM),
        scratch_shapes=[
            pltpu.SMEM(stride_owner.shape[::-1], jnp.int32),
            pltpu.VMEM((2, 2 * rows) + tile, low),
            pltpu.VMEM((2, rows) + tile, low),
            pltpu.VMEM((2 * rows,) + tile, wide),
            pltpu.VMEM((2 * rows,) + tile, wide),
            pltpu.VMEM((rows * PICKS + 1,) + tile, low),
            pltpu.VMEM((rows * PICKS + 1,) + tile, low),
            pltpu.VMEM((4, rows) + tile, low),
            pltpu.VMEM((2, rows) + tile, low),
            pltpu.VMEM((2, rows) + tile, low),
            dma((1,)),
            dma((1,)),
            dma((n_z,)),
            dma((n_z,)),
            dma((1,)),
            dma((1,)),
            dma((1,)),
            dma((1,)),
            dma((1,)),
            dma((1,)),
            pltpu.SemaphoreType.REGULAR((max(1, rounds - 1),)),
        ],
        compiler_params=pltpu.CompilerParams(
            collective_id=0, has_side_effects=True, vmem_limit_bytes=67043328 - out_bytes
        ),
    )(stride_owner.T, queries, keys, values, grad_out)
    out = jax.ShapeDtypeStruct((n_head, BLOCK, width), low)
    settled = pl.pallas_call(
        partial(settle_kernel, 4, n_head),
        out_shape=(out,) * 4,
        in_specs=[pl.BlockSpec(memory_space=pltpu.VMEM)],
        out_specs=(pl.BlockSpec(memory_space=pl.ANY),) * 4,
        scratch_shapes=[dma((1,))],
        compiler_params=pltpu.CompilerParams(vmem_limit_bytes=8 << 20),
    )(arrived)
    return tuple(part.reshape(seq_rows, width) for part in settled)


def on_device(queries, keys, values, grad_out, stride_owner):
    n_head, n_blk = lax.axis_size("head"), lax.axis_size("blk")
    rows, width = queries.shape
    whole_heads = n_blk % 2 == 0 and width == n_head * (n_blk // 2) * HEAD_DIM
    if rows == BLOCK and whole_heads and n_head & (n_head - 1) == 0:
        return by_heads(queries, keys, values, grad_out, stride_owner)
    return by_runs(queries, keys, values, grad_out, stride_owner)


def solution(mesh):
    return jax.shard_map(
        on_device,
        mesh=mesh,
        in_specs=(
            P(("blk", "head"), None),
            P(("blk", "head"), None),
            P(("blk", "head"), None),
            P(("blk", "head"), None),
            P(),
        ),
        out_specs=(P("blk", "head"), P("blk", "head"), P("blk", "head"), P("blk", "head")),
        check_vma=False,
    )
```

```python
import math
from functools import partial

import jax
import jax.numpy as jnp
from jax import lax
from jax.experimental import pallas as pl
from jax.experimental.pallas import tpu as pltpu
from jax.sharding import PartitionSpec as P

HEAD_DIM = 128
BLOCK = 128
PICKS = 3
MESH = pl.DeviceIdType.MESH


def with_halo(block, sides, width):
    for axis, dim in sides:
        count = lax.axis_size(axis)
        forward = [(i, i + 1) for i in range(count - 1)]
        forward.append((count - 1, 0))
        backward = [(target, source) for source, target in forward]
        low = lax.ppermute(
            lax.slice_in_dim(block, block.shape[dim] - width, None, axis=dim), axis, forward
        )
        high = lax.ppermute(lax.slice_in_dim(block, 0, width, axis=dim), axis, backward)
        block = jnp.concatenate([low, block, high], axis=dim)
    return block


def from_root(block, axis, holder):
    block = jnp.where(lax.axis_index(axis) == holder, block, jnp.zeros_like(block))
    return lax.psum(block, axis)


def slot_tables(stride_owner, n_blk, blocks, capacity, device):
    owner_table = stride_owner.reshape(n_blk, blocks, PICKS)
    owner_ids = jnp.arange(n_blk, dtype=jnp.int32)
    naming = jnp.any(owner_table[:, :, :, None] == owner_ids[None, None, None, :], axis=2)
    counts = naming.astype(jnp.int32)
    ranking = jnp.cumsum(counts, axis=1) - counts
    naming_here = lax.dynamic_index_in_dim(naming, device, 2, keepdims=False)
    ranking_here = lax.dynamic_index_in_dim(ranking, device, 2, keepdims=False)
    slot_ids = jnp.arange(capacity, dtype=jnp.int32)
    matched = naming_here[:, None, :] & (ranking_here[:, None, :] == slot_ids[None, :, None])
    offsets = jnp.sum(
        matched.astype(jnp.int32) * jnp.arange(blocks, dtype=jnp.int32)[None, None, :], axis=2
    )
    own_rows = lax.dynamic_index_in_dim(owner_table, device, 0, keepdims=False)
    own_ranks = lax.dynamic_index_in_dim(ranking, device, 0, keepdims=False)
    picked = jnp.take_along_axis(own_ranks, own_rows, axis=1)
    flat_slot = own_rows * capacity + picked
    return (offsets.reshape(-1), flat_slot, matched.reshape(n_blk * capacity, blocks))


def fetch_keys(stacked, offsets, flat_slot, capacity):
    seq_rows = stacked.shape[1]
    width = stacked.shape[2]
    blocks = seq_rows // BLOCK
    n_blk = lax.axis_size("blk")
    extended = with_halo(stacked, (("blk", 1),), BLOCK)
    extended = extended.reshape(2, blocks + 2, BLOCK, width)
    block_view = stacked.reshape(2, blocks, BLOCK, width)
    leading = from_root(block_view[:, 0:2], "blk", 0)
    outgoing = jnp.take(block_view, offsets, axis=1).reshape(2, n_blk, capacity, BLOCK, width)
    incoming = lax.all_to_all(outgoing, "blk", split_axis=1, concat_axis=1, tiled=True)
    incoming = incoming.reshape(2, n_blk * capacity, BLOCK, width)
    pooled = jnp.concatenate([extended, incoming, leading], axis=1)
    rows_here = jnp.arange(blocks, dtype=jnp.int32)[:, None]
    nearby_index = rows_here + jnp.arange(3, dtype=jnp.int32)[None, :]
    distant_index = blocks + 2 + flat_slot
    leading_index = (
        jnp.zeros((blocks, 2), jnp.int32)
        + (blocks + 2 + n_blk * capacity)
        + jnp.arange(2, dtype=jnp.int32)[None, :]
    )
    table = jnp.concatenate([nearby_index, distant_index, leading_index], axis=1)
    return jnp.take(pooled, table.reshape(-1), axis=1)


def score_block(query_part, key_part, factor):
    return (
        jnp.einsum("gqhd,gjkhd->ghqjk", query_part, key_part, preferred_element_type=jnp.float32)
        * factor
    )


def log_normal(scores):
    row_max = jnp.max(scores, axis=(3, 4), keepdims=True)
    return row_max + jnp.log(jnp.sum(jnp.exp(scores - row_max), axis=(3, 4), keepdims=True))


def output_of(rounded, value_part):
    return jnp.einsum(
        "ghqjk,gjkhd->gqhd", rounded, value_part, preferred_element_type=jnp.float32
    ).astype(jnp.bfloat16)


def split_terms(coeffs, source):
    group_size = source.shape[0]
    near = jnp.einsum(
        "ghqjk,gqhd->gjkhd", coeffs[:, :, :, 0:3], source, preferred_element_type=jnp.float32
    )
    far = jnp.einsum(
        "ghqjk,gqhd->gjkhd", coeffs[:, :, :, 3:6], source, preferred_element_type=jnp.float32
    ).astype(jnp.bfloat16)
    lead = jnp.einsum(
        "ghqjk,gqhd->jkhd", coeffs[:, :, :, 6:8], source, preferred_element_type=jnp.float32
    )
    near = near.reshape(group_size, 3, near.shape[2], near.shape[3] * near.shape[4])
    far = far.reshape(group_size, 3, far.shape[2], far.shape[3] * far.shape[4])
    lead = lead.reshape(2, lead.shape[1], lead.shape[2] * lead.shape[3])
    return (near, far, lead)


def backward_from(
    scores, log_total, rounded, attended, grad_part, query_part, key_part, value_part, factor
):
    grad_weights = jnp.einsum(
        "gqhd,gjkhd->ghqjk", grad_part, value_part, preferred_element_type=jnp.float32
    )
    delta = jnp.sum(grad_part.astype(jnp.float32) * attended.astype(jnp.float32), axis=3)
    delta = jnp.transpose(delta, (0, 2, 1))[:, :, :, None, None]
    grad_scores = (jnp.exp(scores - log_total) * (grad_weights - delta) * factor).astype(
        jnp.bfloat16
    )
    grad_query = jnp.einsum(
        "ghqjk,gjkhd->gqhd", grad_scores, key_part, preferred_element_type=jnp.float32
    ).astype(jnp.bfloat16)
    key_near, key_far, key_lead = split_terms(grad_scores, query_part)
    value_near, value_far, value_lead = split_terms(rounded, grad_part)
    return (grad_query, key_near, key_far, key_lead, value_near, value_far, value_lead)


def spread_near(near_terms, width):
    blank = jnp.zeros((1, BLOCK, width), jnp.float32)
    return (
        jnp.concatenate([near_terms[:, 0], blank, blank], axis=0)
        + jnp.concatenate([blank, near_terms[:, 1], blank], axis=0)
        + jnp.concatenate([blank, blank, near_terms[:, 2]], axis=0)
    )


def by_runs(queries, keys, values, grad_out, stride_owner):
    query_rows, key_rows, value_rows, grad_rows = (
        lax.all_to_all(queries, "head", split_axis=1, concat_axis=0, tiled=True),
        lax.all_to_all(keys, "head", split_axis=1, concat_axis=0, tiled=True),
        lax.all_to_all(values, "head", split_axis=1, concat_axis=0, tiled=True),
        lax.all_to_all(grad_out, "head", split_axis=1, concat_axis=0, tiled=True),
    )
    seq_rows, width = query_rows.shape
    heads_here = width // HEAD_DIM
    blocks = seq_rows // BLOCK
    n_blk = lax.axis_size("blk")
    capacity = max(2, (PICKS * blocks + n_blk - 1) // n_blk)
    device = lax.axis_index("blk")
    offsets, flat_slot, matched = slot_tables(stride_owner, n_blk, blocks, capacity, device)
    group_size = math.gcd(blocks, max(1, 512 // BLOCK))
    group_count = blocks // group_size
    factor = HEAD_DIM ** (-0.5)
    stacked = jnp.stack([key_rows, value_rows])
    query_view = query_rows.reshape(blocks, BLOCK, heads_here, HEAD_DIM)
    grad_view = grad_rows.reshape(blocks, BLOCK, heads_here, HEAD_DIM)
    key_sets = fetch_keys(stacked, offsets, flat_slot, capacity)
    key_sets = key_sets.reshape(2, blocks, 8, BLOCK, heads_here, HEAD_DIM)

    def pieces(group_id):
        start = group_id * group_size
        query_part = lax.dynamic_slice_in_dim(query_view, start, group_size, 0)
        grad_part = lax.dynamic_slice_in_dim(grad_view, start, group_size, 0)
        kv_part = lax.dynamic_slice_in_dim(key_sets, start, group_size, 1)
        return (query_part, grad_part, kv_part[0], kv_part[1])

    def joined_pass(group_id):
        query_part, grad_part, key_part, value_part = pieces(group_id)
        scores = score_block(query_part, key_part, factor)
        log_total = log_normal(scores)
        rounded = jnp.exp(scores - log_total).astype(jnp.bfloat16)
        attended = output_of(rounded, value_part)
        extra = backward_from(
            scores,
            log_total,
            rounded,
            attended,
            grad_part,
            query_part,
            key_part,
            value_part,
            factor,
        )
        return (attended,) + extra

    group_ids = jnp.arange(group_count, dtype=jnp.int32)
    results = lax.map(joined_pass, group_ids)
    attended = results[0]
    grad_query, key_near, key_far, key_lead, value_near, value_far, value_lead = results[1:]
    key_ext = spread_near(key_near.reshape(blocks, 3, BLOCK, width), width)
    value_ext = spread_near(value_near.reshape(blocks, 3, BLOCK, width), width)
    rim_terms = jnp.stack(
        [
            jnp.stack([key_ext[0], value_ext[0]]),
            jnp.stack([key_ext[blocks + 1], value_ext[blocks + 1]]),
        ]
    )
    beside = with_halo(rim_terms.astype(jnp.bfloat16), (("blk", 0),), 1).astype(rim_terms.dtype)
    key_owned = key_ext[1 : blocks + 1].at[0].add(beside[0, 0]).at[blocks - 1].add(beside[3, 0])
    value_owned = value_ext[1 : blocks + 1].at[0].add(beside[0, 1]).at[blocks - 1].add(beside[3, 1])
    slot_flat = flat_slot.reshape(-1)
    key_back = (
        jnp.zeros((n_blk * capacity, BLOCK, width), jnp.bfloat16)
        .at[slot_flat]
        .set(key_far.reshape(blocks * PICKS, BLOCK, width))
    )
    value_back = (
        jnp.zeros((n_blk * capacity, BLOCK, width), jnp.bfloat16)
        .at[slot_flat]
        .set(value_far.reshape(blocks * PICKS, BLOCK, width))
    )
    key_arrived, value_arrived = (
        lax.all_to_all(
            key_back.reshape(n_blk, capacity, BLOCK, width),
            "blk",
            split_axis=0,
            concat_axis=0,
            tiled=True,
        ),
        lax.all_to_all(
            value_back.reshape(n_blk, capacity, BLOCK, width),
            "blk",
            split_axis=0,
            concat_axis=0,
            tiled=True,
        ),
    )
    match_b = matched.astype(jnp.bfloat16)
    key_owned = key_owned + jnp.einsum(
        "sr,sbc->rbc",
        match_b,
        key_arrived.reshape(n_blk * capacity, BLOCK, width),
        preferred_element_type=jnp.float32,
    )
    value_owned = value_owned + jnp.einsum(
        "sr,sbc->rbc",
        match_b,
        value_arrived.reshape(n_blk * capacity, BLOCK, width),
        preferred_element_type=jnp.float32,
    )
    key_total, value_total = (
        lax.psum(jnp.sum(key_lead, axis=0).astype(jnp.bfloat16), "blk").astype(jnp.float32),
        lax.psum(jnp.sum(value_lead, axis=0).astype(jnp.bfloat16), "blk").astype(jnp.float32),
    )
    at_root = device == 0
    key_owned = key_owned.at[0:2].add(jnp.where(at_root, key_total, jnp.zeros_like(key_total)))
    value_owned = value_owned.at[0:2].add(
        jnp.where(at_root, value_total, jnp.zeros_like(value_total))
    )
    grad_keys = key_owned.astype(jnp.bfloat16).reshape(seq_rows, width)
    grad_values = value_owned.astype(jnp.bfloat16).reshape(seq_rows, width)
    return (
        attended.reshape(seq_rows, width),
        grad_query.reshape(seq_rows, width),
        grad_keys,
        grad_values,
    )


def head_bits(n_head):
    return [1 << bit for bit in range(n_head.bit_length() - 1)]


def neighbours(n_head, n_z, at_z):
    beside = [(at_z, flip, 0) for flip in head_bits(n_head)] + [(at_z, 0, 1)]
    return beside + [(z2, 0, 0) for z2 in (at_z - 1, at_z + 1) if 0 <= z2 < n_z]


def seen_from(peer, at_z):
    return (at_z, peer[1], peer[2])


def entry_rounds(n_head, n_z):
    middle = n_z // 2
    hears, knows = [], []
    near = [neighbours(n_head, n_z, at_z) for at_z in range(n_z)]
    first = [set(near[at_z]) for at_z in range(n_z)]
    if middle:
        first[middle] = {(middle - 1, 0, 0)}
    hears.append(first)
    knows.append([{(at_z, 0, 0)} | first[at_z] for at_z in range(n_z)])
    reached = [
        {(z2, flips, 0) for z2 in range(n_z) for flips in range(n_head)} | {(at_z, 0, 1)}
        for at_z in range(n_z)
    ]
    while any(want - known for want, known in zip(reached, knows[-1])):
        known = knows[-1]
        heard = [
            {p for p in near[at_z] if seen_from(p, at_z) in known[p[0]]} for at_z in range(n_z)
        ]
        hears.append(heard)
        knows.append(
            [
                known[at_z].union(
                    *(
                        {(k[0], k[1] ^ p[1], k[2] ^ p[2]) for k in known[p[0]]}
                        for p in heard[at_z]
                    )
                )
                for at_z in range(n_z)
            ]
        )
    return hears, knows


def head_kernel(
    n_head,
    n_z,
    owner_in,
    q_in,
    k_in,
    v_in,
    g_in,
    out,
    owner_ref,
    kv_all,
    qg_all,
    k_sum,
    v_sum,
    k_far,
    v_far,
    stage,
    give,
    take,
    owner_sem,
    in_send,
    kv_recv,
    qg_recv,
    pass_send,
    pass_recv,
    pair_send,
    pair_recv,
    out_send,
    out_recv,
    near_sem,
):
    head = lax.axis_index("head")
    blk = lax.axis_index("blk")
    z = blk // 2
    c = blk % 2
    runs = n_head
    total_blocks = 2 * n_z * runs
    factor = HEAD_DIM ** (-0.5)
    my_head = head * n_z + z
    mine = blk * runs + head
    my_row = z * runs + head
    sibling = {"head": head, "blk": 2 * z + 1 - c}

    def columns(head_id):
        return pl.ds(pl.multiple_of(head_id * HEAD_DIM, HEAD_DIM), HEAD_DIM)

    bits = head_bits(n_head)
    hears, knows = entry_rounds(n_head, n_z)
    barrier = pltpu.get_barrier_semaphore()

    def flipped(flips):
        moved = head
        for flip in bits:
            if flips & flip:
                moved = moved + flip - 2 * flip * ((head // flip) % 2)
        return moved

    def place(peer):
        at_z, flips, other = peer
        return {"head": flipped(flips), "blk": 2 * at_z + (1 - c if other else c)}

    def greet(at_z, step):
        sem = barrier if step == 0 else near_sem.at[step - 1]
        for peer in neighbours(n_head, n_z, at_z):
            if seen_from(peer, at_z) in hears[step][peer[0]]:
                pl.semaphore_signal(sem, inc=1, device_id=place(peer), device_id_type=MESH)

    def hear(at_z, step):
        sem = barrier if step == 0 else near_sem.at[step - 1]
        if hears[step][at_z]:
            pl.semaphore_wait(sem, len(hears[step][at_z]))

    def push(sources, target, slot, recv_sem, at_z, peer):
        z2, flips, _ = peer
        for at, source in enumerate(sources):
            pltpu.make_async_remote_copy(
                src_ref=source.at[:, columns(flipped(flips) * n_z + z2)],
                dst_ref=target.at[at, slot],
                send_sem=in_send.at[0],
                recv_sem=recv_sem.at[(z2 + n_z - at_z) % n_z],
                device_id=place(peer),
                device_id_type=MESH,
            ).start()

    def crosses(at_z, peer):
        return (at_z < n_z // 2) != (peer[0] < n_z // 2)

    def urgency(at_z, peer):
        hops = abs(peer[0] - at_z) + bin(peer[1]).count("1")
        return (not crosses(at_z, peer), hops, peer)

    def enter(at_z):
        greet(at_z, 0)
        local = [pltpu.make_async_copy(owner_in, owner_ref, owner_sem.at[0])]
        for sources, target, slot, sem in (
            ((k_in, v_in), kv_all, mine, kv_recv),
            ((q_in, g_in), qg_all, my_row, qg_recv),
        ):
            for at, source in enumerate(sources):
                local.append(
                    pltpu.make_async_copy(
                        source.at[:, columns(my_head)], target.at[at, slot], sem.at[0]
                    )
                )
        for copy in local:
            copy.start()
        early = []
        met = {(at_z, 0, 0)}
        for step in range(len(hears)):
            hear(at_z, step)
            fresh = [p for p in knows[step][at_z] - met if not p[2]]
            met |= knows[step][at_z]
            fresh.sort(key=partial(urgency, at_z))
            first = [p for p in fresh if step == 0 and crosses(at_z, p)]
            for peer in first:
                push((k_in, v_in), kv_all, mine, kv_recv, at_z, peer)
                push((q_in, g_in), qg_all, my_row, qg_recv, at_z, peer)
            early += first
            if step + 1 < len(hears):
                greet(at_z, step + 1)
            for peer in fresh:
                if peer not in first:
                    push((k_in, v_in), kv_all, mine, kv_recv, at_z, peer)
        late = [p for p in met if not p[2] and p[:2] != (at_z, 0) and p not in early]
        for dz in [n_z // 2] + [d for d in range(n_z - 1, -1, -1) if d != n_z // 2]:
            for peer in sorted(late, key=partial(urgency, at_z)):
                if abs(peer[0] - at_z) == dz:
                    push((q_in, g_in), qg_all, my_row, qg_recv, at_z, peer)

    for at_z in range(n_z):
        pl.when(z == at_z)(partial(enter, at_z))

    blank = jnp.zeros((BLOCK, HEAD_DIM), jnp.float32)

    def clear(n, carry):
        k_sum[n] = blank
        v_sum[n] = blank
        return carry

    lax.fori_loop(0, total_blocks, clear, 0)
    none = n_z * runs * PICKS
    k_far[none] = blank.astype(jnp.bfloat16)
    v_far[none] = blank.astype(jnp.bfloat16)

    def await_bytes(ref, sem):
        pltpu.make_async_remote_copy(
            src_ref=ref,
            dst_ref=ref,
            send_sem=sem,
            recv_sem=sem,
            device_id=sibling,
            device_id_type=MESH,
        ).wait_recv()

    def run_of(dz, core):
        return 2 * ((z + n_z - dz) % n_z) + core

    order = [0, 1, n_z - 1] + list(range(2, n_z - 1))
    for dz in order[:n_z]:
        group = kv_all.at[:, pl.ds(run_of(dz, c) * runs, runs)]
        await_bytes(group, kv_recv.at[dz])
        pltpu.make_async_remote_copy(
            src_ref=group,
            dst_ref=group,
            send_sem=pass_send.at[0],
            recv_sem=pass_recv.at[0],
            device_id=sibling,
            device_id_type=MESH,
        ).start()
    pltpu.make_async_copy(owner_in, owner_ref, owner_sem.at[0]).wait()
    await_bytes(qg_all, pass_recv.at[0])

    def contract(left, right, dims):
        return lax.dot_general(
            left, right, ((dims[:1], dims[1:]), ((), ())), preferred_element_type=jnp.float32
        )

    def query_step(z1, r):
        row = z1 * runs + r
        block = (2 * z1 + c) * runs + r
        low = (block + total_blocks - 1) % total_blocks
        high = (block + 1) % total_blocks
        picks = [owner_ref[j, block] * runs + r for j in range(PICKS)]
        named = [low, block, high] + picks + [0, 1]
        keys = jnp.concatenate([kv_all[0, n] for n in named], axis=0)
        values = jnp.concatenate([kv_all[1, n] for n in named], axis=0)
        query = qg_all[0, row]
        grad = qg_all[1, row]
        scores = contract(keys, query, (1, 1))
        top = jnp.max(scores, axis=0, keepdims=True)
        weights = jnp.exp((scores - top) * factor)
        weights = weights * (1.0 / jnp.sum(weights, axis=0, keepdims=True))
        rounded = weights.astype(jnp.bfloat16)
        grad_weights = contract(values, grad, (1, 1))
        delta = jnp.sum(weights * grad_weights, axis=0, keepdims=True)
        grad_scores = (weights * (grad_weights - delta) * factor).astype(jnp.bfloat16)
        stage[0, row] = contract(rounded, values, (0, 0)).astype(jnp.bfloat16)
        stage[1, row] = contract(grad_scores, keys, (0, 0)).astype(jnp.bfloat16)
        key_terms = contract(grad_scores, query, (1, 0))
        value_terms = contract(rounded, grad, (1, 0))
        for j, n in ((0, low), (1, block), (2, high), (6, 0), (7, 1)):
            k_sum[n] += key_terms[j * BLOCK : (j + 1) * BLOCK]
            v_sum[n] += value_terms[j * BLOCK : (j + 1) * BLOCK]
        for j in range(PICKS):
            rows = slice((3 + j) * BLOCK, (4 + j) * BLOCK)
            k_far[row * PICKS + j] = key_terms[rows].astype(jnp.bfloat16)
            v_far[row * PICKS + j] = value_terms[rows].astype(jnp.bfloat16)

    def hand_out(first, dz):
        z2 = (z + n_z - dz) % n_z
        source = stage.at[pl.ds(first, 2), pl.ds(z2 * runs, runs)]
        target = out.at[pl.ds(first, 2), :, :, columns(z)]
        if dz == 0:
            pltpu.make_async_copy(source, target, out_recv.at[0]).start()
        else:
            pltpu.make_async_remote_copy(
                src_ref=source,
                dst_ref=target,
                send_sem=out_send.at[0],
                recv_sem=out_recv.at[0],
                device_id={"head": head, "blk": 2 * z2 + c},
                device_id_type=MESH,
            ).start()

    def await_sent(ref, sem):
        pltpu.make_async_remote_copy(
            src_ref=ref,
            dst_ref=ref,
            send_sem=sem,
            recv_sem=sem,
            device_id=sibling,
            device_id_type=MESH,
        ).wait_send()

    rows = n_z * runs
    far_first = [dz for dz in (2, 1, 3, 0) if dz < n_z] + list(range(4, n_z))
    for dz in far_first:
        z1 = (z + n_z - dz) % n_z
        await_bytes(qg_all.at[:, pl.ds(z1 * runs, runs)], qg_recv.at[dz])

        def step(r, carry, z1=z1):
            query_step(z1, r)
            return carry

        lax.fori_loop(0, runs, step, 0)
        if dz == far_first[0]:
            await_sent(kv_all.at[:, pl.ds(0, 2 * (rows - 1))], in_send.at[0])
        hand_out(0, dz)

    def total_of(sums, far, run, r):
        total = sums[run * runs + r]
        for z1 in range(n_z):
            block = (2 * z1 + c) * runs + r
            row = z1 * runs + r
            place = none
            for j in range(PICKS):
                place = jnp.where(owner_ref[j, block] == run, row * PICKS + j, place)
            total = total + far[place].astype(jnp.float32)
        return total

    def give_step(row, carry):
        run, r = 2 * (row // runs) + 1 - c, row % runs
        give[0, row] = total_of(k_sum, k_far, run, r).astype(jnp.bfloat16)
        give[1, row] = total_of(v_sum, v_far, run, r).astype(jnp.bfloat16)
        return carry

    lax.fori_loop(0, n_z * runs, give_step, 0)
    pair = pltpu.make_async_remote_copy(
        src_ref=give,
        dst_ref=take,
        send_sem=pair_send.at[0],
        recv_sem=pair_recv.at[0],
        device_id=sibling,
        device_id_type=MESH,
    )
    pair.start()
    pair.wait_recv()
    for dz in far_first:
        z1 = (z + n_z - dz) % n_z

        def join_step(r, carry, z1=z1):
            row, run = z1 * runs + r, 2 * z1 + c
            for at, sums, far in ((0, k_sum, k_far), (1, v_sum, v_far)):
                total = total_of(sums, far, run, r) + take[at, row].astype(jnp.float32)
                stage[2 + at, row] = total.astype(jnp.bfloat16)
            return carry

        lax.fori_loop(0, runs, join_step, 0)
        hand_out(2, dz)

    pair.wait_send()
    await_sent(qg_all, pass_send.at[0])
    if n_z > 1:
        await_sent(kv_all.at[:, pl.ds(0, 2 * (rows - runs))], out_send.at[0])
    await_bytes(out, out_recv.at[0])


def settle_kernel(count, pieces, source, *refs):
    targets, sem = refs[:count], refs[count]
    copies = [
        pltpu.make_async_copy(
            source.at[at, piece], targets[at].at[piece], sem.at[0]
        )
        for at in range(count)
        for piece in range(pieces)
    ]
    for copy in copies:
        copy.start()
    pltpu.make_async_copy(source, source, sem.at[0]).wait()


def by_heads(queries, keys, values, grad_out, stride_owner):
    n_head, n_blk = lax.axis_size("head"), lax.axis_size("blk")
    n_z = n_blk // 2
    rows = n_z * n_head
    rounds = len(entry_rounds(n_head, n_z)[0])
    seq_rows, width = BLOCK * n_head, n_z * HEAD_DIM
    tile = (BLOCK, HEAD_DIM)
    low, wide = jnp.bfloat16, jnp.float32
    dma = pltpu.SemaphoreType.DMA
    out_bytes = 8 * seq_rows * width
    arrived = pl.pallas_call(
        partial(head_kernel, n_head, n_z),
        out_shape=pltpu.VMEM((4, n_head, BLOCK, width), low),
        in_specs=[pl.BlockSpec(memory_space=pltpu.HBM)] * 5,
        out_specs=pl.BlockSpec(memory_space=pltpu.VMEM),
        scratch_shapes=[
            pltpu.SMEM(stride_owner.shape[::-1], jnp.int32),
            pltpu.VMEM((2, 2 * rows) + tile, low),
            pltpu.VMEM((2, rows) + tile, low),
            pltpu.VMEM((2 * rows,) + tile, wide),
            pltpu.VMEM((2 * rows,) + tile, wide),
            pltpu.VMEM((rows * PICKS + 1,) + tile, low),
            pltpu.VMEM((rows * PICKS + 1,) + tile, low),
            pltpu.VMEM((4, rows) + tile, low),
            pltpu.VMEM((2, rows) + tile, low),
            pltpu.VMEM((2, rows) + tile, low),
            dma((1,)),
            dma((1,)),
            dma((n_z,)),
            dma((n_z,)),
            dma((1,)),
            dma((1,)),
            dma((1,)),
            dma((1,)),
            dma((1,)),
            dma((1,)),
            pltpu.SemaphoreType.REGULAR((max(1, rounds - 1),)),
        ],
        compiler_params=pltpu.CompilerParams(
            collective_id=0, has_side_effects=True, vmem_limit_bytes=67043328 - out_bytes
        ),
    )(stride_owner.T, queries, keys, values, grad_out)
    out = jax.ShapeDtypeStruct((n_head, BLOCK, width), low)
    settled = pl.pallas_call(
        partial(settle_kernel, 4, n_head),
        out_shape=(out,) * 4,
        in_specs=[pl.BlockSpec(memory_space=pltpu.VMEM)],
        out_specs=(pl.BlockSpec(memory_space=pl.ANY),) * 4,
        scratch_shapes=[dma((1,))],
        compiler_params=pltpu.CompilerParams(vmem_limit_bytes=8 << 20),
    )(arrived)
    return tuple(part.reshape(seq_rows, width) for part in settled)


def on_device(queries, keys, values, grad_out, stride_owner):
    n_head, n_blk = lax.axis_size("head"), lax.axis_size("blk")
    rows, width = queries.shape
    whole_heads = n_blk % 2 == 0 and width == n_head * (n_blk // 2) * HEAD_DIM
    if rows == BLOCK and whole_heads and n_head & (n_head - 1) == 0:
        return by_heads(queries, keys, values, grad_out, stride_owner)
    return by_runs(queries, keys, values, grad_out, stride_owner)


def solution(mesh):
    return jax.shard_map(
        on_device,
        mesh=mesh,
        in_specs=(
            P(("blk", "head"), None),
            P(("blk", "head"), None),
            P(("blk", "head"), None),
            P(("blk", "head"), None),
            P(),
        ),
        out_specs=(P("blk", "head"), P("blk", "head"), P("blk", "head"), P("blk", "head")),
        check_vma=False,
    )
```

```python
import math
from functools import partial

import jax
import jax.numpy as jnp
from jax import lax
from jax.experimental import pallas as pl
from jax.experimental.pallas import tpu as pltpu
from jax.sharding import PartitionSpec as P

HEAD_DIM = 128
BLOCK = 128
PICKS = 3
MESH = pl.DeviceIdType.MESH


def with_halo(block, sides, width):
    for axis, dim in sides:
        count = lax.axis_size(axis)
        forward = [(i, i + 1) for i in range(count - 1)]
        forward.append((count - 1, 0))
        backward = [(target, source) for source, target in forward]
        low = lax.ppermute(
            lax.slice_in_dim(block, block.shape[dim] - width, None, axis=dim), axis, forward
        )
        high = lax.ppermute(lax.slice_in_dim(block, 0, width, axis=dim), axis, backward)
        block = jnp.concatenate([low, block, high], axis=dim)
    return block


def from_root(block, axis, holder):
    block = jnp.where(lax.axis_index(axis) == holder, block, jnp.zeros_like(block))
    return lax.psum(block, axis)


def slot_tables(stride_owner, n_blk, blocks, capacity, device):
    owner_table = stride_owner.reshape(n_blk, blocks, PICKS)
    owner_ids = jnp.arange(n_blk, dtype=jnp.int32)
    naming = jnp.any(owner_table[:, :, :, None] == owner_ids[None, None, None, :], axis=2)
    counts = naming.astype(jnp.int32)
    ranking = jnp.cumsum(counts, axis=1) - counts
    naming_here = lax.dynamic_index_in_dim(naming, device, 2, keepdims=False)
    ranking_here = lax.dynamic_index_in_dim(ranking, device, 2, keepdims=False)
    slot_ids = jnp.arange(capacity, dtype=jnp.int32)
    matched = naming_here[:, None, :] & (ranking_here[:, None, :] == slot_ids[None, :, None])
    offsets = jnp.sum(
        matched.astype(jnp.int32) * jnp.arange(blocks, dtype=jnp.int32)[None, None, :], axis=2
    )
    own_rows = lax.dynamic_index_in_dim(owner_table, device, 0, keepdims=False)
    own_ranks = lax.dynamic_index_in_dim(ranking, device, 0, keepdims=False)
    picked = jnp.take_along_axis(own_ranks, own_rows, axis=1)
    flat_slot = own_rows * capacity + picked
    return (offsets.reshape(-1), flat_slot, matched.reshape(n_blk * capacity, blocks))


def fetch_keys(stacked, offsets, flat_slot, capacity):
    seq_rows = stacked.shape[1]
    width = stacked.shape[2]
    blocks = seq_rows // BLOCK
    n_blk = lax.axis_size("blk")
    extended = with_halo(stacked, (("blk", 1),), BLOCK)
    extended = extended.reshape(2, blocks + 2, BLOCK, width)
    block_view = stacked.reshape(2, blocks, BLOCK, width)
    leading = from_root(block_view[:, 0:2], "blk", 0)
    outgoing = jnp.take(block_view, offsets, axis=1).reshape(2, n_blk, capacity, BLOCK, width)
    incoming = lax.all_to_all(outgoing, "blk", split_axis=1, concat_axis=1, tiled=True)
    incoming = incoming.reshape(2, n_blk * capacity, BLOCK, width)
    pooled = jnp.concatenate([extended, incoming, leading], axis=1)
    rows_here = jnp.arange(blocks, dtype=jnp.int32)[:, None]
    nearby_index = rows_here + jnp.arange(3, dtype=jnp.int32)[None, :]
    distant_index = blocks + 2 + flat_slot
    leading_index = (
        jnp.zeros((blocks, 2), jnp.int32)
        + (blocks + 2 + n_blk * capacity)
        + jnp.arange(2, dtype=jnp.int32)[None, :]
    )
    table = jnp.concatenate([nearby_index, distant_index, leading_index], axis=1)
    return jnp.take(pooled, table.reshape(-1), axis=1)


def score_block(query_part, key_part, factor):
    return (
        jnp.einsum("gqhd,gjkhd->ghqjk", query_part, key_part, preferred_element_type=jnp.float32)
        * factor
    )


def log_normal(scores):
    row_max = jnp.max(scores, axis=(3, 4), keepdims=True)
    return row_max + jnp.log(jnp.sum(jnp.exp(scores - row_max), axis=(3, 4), keepdims=True))


def output_of(rounded, value_part):
    return jnp.einsum(
        "ghqjk,gjkhd->gqhd", rounded, value_part, preferred_element_type=jnp.float32
    ).astype(jnp.bfloat16)


def split_terms(coeffs, source):
    group_size = source.shape[0]
    near = jnp.einsum(
        "ghqjk,gqhd->gjkhd", coeffs[:, :, :, 0:3], source, preferred_element_type=jnp.float32
    )
    far = jnp.einsum(
        "ghqjk,gqhd->gjkhd", coeffs[:, :, :, 3:6], source, preferred_element_type=jnp.float32
    ).astype(jnp.bfloat16)
    lead = jnp.einsum(
        "ghqjk,gqhd->jkhd", coeffs[:, :, :, 6:8], source, preferred_element_type=jnp.float32
    )
    near = near.reshape(group_size, 3, near.shape[2], near.shape[3] * near.shape[4])
    far = far.reshape(group_size, 3, far.shape[2], far.shape[3] * far.shape[4])
    lead = lead.reshape(2, lead.shape[1], lead.shape[2] * lead.shape[3])
    return (near, far, lead)


def backward_from(
    scores, log_total, rounded, attended, grad_part, query_part, key_part, value_part, factor
):
    grad_weights = jnp.einsum(
        "gqhd,gjkhd->ghqjk", grad_part, value_part, preferred_element_type=jnp.float32
    )
    delta = jnp.sum(grad_part.astype(jnp.float32) * attended.astype(jnp.float32), axis=3)
    delta = jnp.transpose(delta, (0, 2, 1))[:, :, :, None, None]
    grad_scores = (jnp.exp(scores - log_total) * (grad_weights - delta) * factor).astype(
        jnp.bfloat16
    )
    grad_query = jnp.einsum(
        "ghqjk,gjkhd->gqhd", grad_scores, key_part, preferred_element_type=jnp.float32
    ).astype(jnp.bfloat16)
    key_near, key_far, key_lead = split_terms(grad_scores, query_part)
    value_near, value_far, value_lead = split_terms(rounded, grad_part)
    return (grad_query, key_near, key_far, key_lead, value_near, value_far, value_lead)


def spread_near(near_terms, width):
    blank = jnp.zeros((1, BLOCK, width), jnp.float32)
    return (
        jnp.concatenate([near_terms[:, 0], blank, blank], axis=0)
        + jnp.concatenate([blank, near_terms[:, 1], blank], axis=0)
        + jnp.concatenate([blank, blank, near_terms[:, 2]], axis=0)
    )


def by_runs(queries, keys, values, grad_out, stride_owner):
    query_rows, key_rows, value_rows, grad_rows = (
        lax.all_to_all(queries, "head", split_axis=1, concat_axis=0, tiled=True),
        lax.all_to_all(keys, "head", split_axis=1, concat_axis=0, tiled=True),
        lax.all_to_all(values, "head", split_axis=1, concat_axis=0, tiled=True),
        lax.all_to_all(grad_out, "head", split_axis=1, concat_axis=0, tiled=True),
    )
    seq_rows, width = query_rows.shape
    heads_here = width // HEAD_DIM
    blocks = seq_rows // BLOCK
    n_blk = lax.axis_size("blk")
    capacity = max(2, (PICKS * blocks + n_blk - 1) // n_blk)
    device = lax.axis_index("blk")
    offsets, flat_slot, matched = slot_tables(stride_owner, n_blk, blocks, capacity, device)
    group_size = math.gcd(blocks, max(1, 512 // BLOCK))
    group_count = blocks // group_size
    factor = HEAD_DIM ** (-0.5)
    stacked = jnp.stack([key_rows, value_rows])
    query_view = query_rows.reshape(blocks, BLOCK, heads_here, HEAD_DIM)
    grad_view = grad_rows.reshape(blocks, BLOCK, heads_here, HEAD_DIM)
    key_sets = fetch_keys(stacked, offsets, flat_slot, capacity)
    key_sets = key_sets.reshape(2, blocks, 8, BLOCK, heads_here, HEAD_DIM)

    def pieces(group_id):
        start = group_id * group_size
        query_part = lax.dynamic_slice_in_dim(query_view, start, group_size, 0)
        grad_part = lax.dynamic_slice_in_dim(grad_view, start, group_size, 0)
        kv_part = lax.dynamic_slice_in_dim(key_sets, start, group_size, 1)
        return (query_part, grad_part, kv_part[0], kv_part[1])

    def joined_pass(group_id):
        query_part, grad_part, key_part, value_part = pieces(group_id)
        scores = score_block(query_part, key_part, factor)
        log_total = log_normal(scores)
        rounded = jnp.exp(scores - log_total).astype(jnp.bfloat16)
        attended = output_of(rounded, value_part)
        extra = backward_from(
            scores,
            log_total,
            rounded,
            attended,
            grad_part,
            query_part,
            key_part,
            value_part,
            factor,
        )
        return (attended,) + extra

    group_ids = jnp.arange(group_count, dtype=jnp.int32)
    results = lax.map(joined_pass, group_ids)
    attended = results[0]
    grad_query, key_near, key_far, key_lead, value_near, value_far, value_lead = results[1:]
    key_ext = spread_near(key_near.reshape(blocks, 3, BLOCK, width), width)
    value_ext = spread_near(value_near.reshape(blocks, 3, BLOCK, width), width)
    rim_terms = jnp.stack(
        [
            jnp.stack([key_ext[0], value_ext[0]]),
            jnp.stack([key_ext[blocks + 1], value_ext[blocks + 1]]),
        ]
    )
    beside = with_halo(rim_terms.astype(jnp.bfloat16), (("blk", 0),), 1).astype(rim_terms.dtype)
    key_owned = key_ext[1 : blocks + 1].at[0].add(beside[0, 0]).at[blocks - 1].add(beside[3, 0])
    value_owned = value_ext[1 : blocks + 1].at[0].add(beside[0, 1]).at[blocks - 1].add(beside[3, 1])
    slot_flat = flat_slot.reshape(-1)
    key_back = (
        jnp.zeros((n_blk * capacity, BLOCK, width), jnp.bfloat16)
        .at[slot_flat]
        .set(key_far.reshape(blocks * PICKS, BLOCK, width))
    )
    value_back = (
        jnp.zeros((n_blk * capacity, BLOCK, width), jnp.bfloat16)
        .at[slot_flat]
        .set(value_far.reshape(blocks * PICKS, BLOCK, width))
    )
    key_arrived, value_arrived = (
        lax.all_to_all(
            key_back.reshape(n_blk, capacity, BLOCK, width),
            "blk",
            split_axis=0,
            concat_axis=0,
            tiled=True,
        ),
        lax.all_to_all(
            value_back.reshape(n_blk, capacity, BLOCK, width),
            "blk",
            split_axis=0,
            concat_axis=0,
            tiled=True,
        ),
    )
    match_b = matched.astype(jnp.bfloat16)
    key_owned = key_owned + jnp.einsum(
        "sr,sbc->rbc",
        match_b,
        key_arrived.reshape(n_blk * capacity, BLOCK, width),
        preferred_element_type=jnp.float32,
    )
    value_owned = value_owned + jnp.einsum(
        "sr,sbc->rbc",
        match_b,
        value_arrived.reshape(n_blk * capacity, BLOCK, width),
        preferred_element_type=jnp.float32,
    )
    key_total, value_total = (
        lax.psum(jnp.sum(key_lead, axis=0).astype(jnp.bfloat16), "blk").astype(jnp.float32),
        lax.psum(jnp.sum(value_lead, axis=0).astype(jnp.bfloat16), "blk").astype(jnp.float32),
    )
    at_root = device == 0
    key_owned = key_owned.at[0:2].add(jnp.where(at_root, key_total, jnp.zeros_like(key_total)))
    value_owned = value_owned.at[0:2].add(
        jnp.where(at_root, value_total, jnp.zeros_like(value_total))
    )
    grad_keys = key_owned.astype(jnp.bfloat16).reshape(seq_rows, width)
    grad_values = value_owned.astype(jnp.bfloat16).reshape(seq_rows, width)
    return (
        attended.reshape(seq_rows, width),
        grad_query.reshape(seq_rows, width),
        grad_keys,
        grad_values,
    )


def head_bits(n_head):
    return [1 << bit for bit in range(n_head.bit_length() - 1)]


def neighbours(n_head, n_z, at_z):
    beside = [(at_z, flip, 0) for flip in head_bits(n_head)] + [(at_z, 0, 1)]
    return beside + [(z2, 0, 0) for z2 in (at_z - 1, at_z + 1) if 0 <= z2 < n_z]


def seen_from(peer, at_z):
    return (at_z, peer[1], peer[2])


def entry_rounds(n_head, n_z):
    middle = n_z // 2
    hears, knows = [], []
    near = [neighbours(n_head, n_z, at_z) for at_z in range(n_z)]
    first = [set(near[at_z]) for at_z in range(n_z)]
    if middle:
        first[middle] = {(middle - 1, 0, 0)}
    hears.append(first)
    knows.append([{(at_z, 0, 0)} | first[at_z] for at_z in range(n_z)])
    reached = [
        {(z2, flips, 0) for z2 in range(n_z) for flips in range(n_head)} | {(at_z, 0, 1)}
        for at_z in range(n_z)
    ]
    while any(want - known for want, known in zip(reached, knows[-1])):
        known = knows[-1]
        heard = [
            {p for p in near[at_z] if seen_from(p, at_z) in known[p[0]]} for at_z in range(n_z)
        ]
        hears.append(heard)
        knows.append(
            [
                known[at_z].union(
                    *(
                        {(k[0], k[1] ^ p[1], k[2] ^ p[2]) for k in known[p[0]]}
                        for p in heard[at_z]
                    )
                )
                for at_z in range(n_z)
            ]
        )
    return hears, knows


def head_kernel(
    n_head,
    n_z,
    owner_in,
    q_in,
    k_in,
    v_in,
    g_in,
    out,
    owner_ref,
    kv_all,
    qg_all,
    k_sum,
    v_sum,
    k_far,
    v_far,
    stage,
    give,
    take,
    owner_sem,
    in_send,
    kv_recv,
    qg_recv,
    pass_send,
    pass_recv,
    pair_send,
    pair_recv,
    out_send,
    out_recv,
    near_sem,
):
    head = lax.axis_index("head")
    blk = lax.axis_index("blk")
    z = blk // 2
    c = blk % 2
    runs = n_head
    total_blocks = 2 * n_z * runs
    factor = HEAD_DIM ** (-0.5)
    my_head = head * n_z + z
    mine = blk * runs + head
    my_row = z * runs + head
    sibling = {"head": head, "blk": 2 * z + 1 - c}

    def columns(head_id):
        return pl.ds(pl.multiple_of(head_id * HEAD_DIM, HEAD_DIM), HEAD_DIM)

    bits = head_bits(n_head)
    hears, knows = entry_rounds(n_head, n_z)
    barrier = pltpu.get_barrier_semaphore()

    def flipped(flips):
        moved = head
        for flip in bits:
            if flips & flip:
                moved = moved + flip - 2 * flip * ((head // flip) % 2)
        return moved

    def place(peer):
        at_z, flips, other = peer
        return {"head": flipped(flips), "blk": 2 * at_z + (1 - c if other else c)}

    def greet(at_z, step):
        sem = barrier if step == 0 else near_sem.at[step - 1]
        for peer in neighbours(n_head, n_z, at_z):
            if seen_from(peer, at_z) in hears[step][peer[0]]:
                pl.semaphore_signal(sem, inc=1, device_id=place(peer), device_id_type=MESH)

    def hear(at_z, step):
        sem = barrier if step == 0 else near_sem.at[step - 1]
        if hears[step][at_z]:
            pl.semaphore_wait(sem, len(hears[step][at_z]))

    def push(sources, target, slot, recv_sem, at_z, peer):
        z2, flips, _ = peer
        for at, source in enumerate(sources):
            pltpu.make_async_remote_copy(
                src_ref=source.at[:, columns(flipped(flips) * n_z + z2)],
                dst_ref=target.at[at, slot],
                send_sem=in_send.at[0],
                recv_sem=recv_sem.at[(z2 + n_z - at_z) % n_z],
                device_id=place(peer),
                device_id_type=MESH,
            ).start()

    def crosses(at_z, peer):
        return (at_z < n_z // 2) != (peer[0] < n_z // 2)

    def urgency(at_z, peer):
        hops = abs(peer[0] - at_z) + bin(peer[1]).count("1")
        return (not crosses(at_z, peer), hops, peer)

    def enter(at_z):
        greet(at_z, 0)
        local = [pltpu.make_async_copy(owner_in, owner_ref, owner_sem.at[0])]
        for sources, target, slot, sem in (
            ((k_in, v_in), kv_all, mine, kv_recv),
            ((q_in, g_in), qg_all, my_row, qg_recv),
        ):
            for at, source in enumerate(sources):
                local.append(
                    pltpu.make_async_copy(
                        source.at[:, columns(my_head)], target.at[at, slot], sem.at[0]
                    )
                )
        for copy in local:
            copy.start()
        early = []
        met = {(at_z, 0, 0)}
        for step in range(len(hears)):
            hear(at_z, step)
            fresh = [p for p in knows[step][at_z] - met if not p[2]]
            met |= knows[step][at_z]
            fresh.sort(key=partial(urgency, at_z))
            first = [p for p in fresh if step == 0 and crosses(at_z, p)]
            for peer in first:
                push((k_in, v_in), kv_all, mine, kv_recv, at_z, peer)
                push((q_in, g_in), qg_all, my_row, qg_recv, at_z, peer)
            early += first
            if step + 1 < len(hears):
                greet(at_z, step + 1)
            for peer in fresh:
                if peer not in first:
                    push((k_in, v_in), kv_all, mine, kv_recv, at_z, peer)
        late = [p for p in met if not p[2] and p[:2] != (at_z, 0) and p not in early]
        for dz in [n_z // 2] + [d for d in range(n_z - 1, -1, -1) if d != n_z // 2]:
            for peer in sorted(late, key=partial(urgency, at_z)):
                if abs(peer[0] - at_z) == dz:
                    push((q_in, g_in), qg_all, my_row, qg_recv, at_z, peer)

    for at_z in range(n_z):
        pl.when(z == at_z)(partial(enter, at_z))

    blank = jnp.zeros((BLOCK, HEAD_DIM), jnp.float32)

    def clear(n, carry):
        k_sum[n] = blank
        v_sum[n] = blank
        return carry

    lax.fori_loop(0, total_blocks, clear, 0)
    none = n_z * runs * PICKS
    k_far[none] = blank.astype(jnp.bfloat16)
    v_far[none] = blank.astype(jnp.bfloat16)

    def await_bytes(ref, sem):
        pltpu.make_async_remote_copy(
            src_ref=ref,
            dst_ref=ref,
            send_sem=sem,
            recv_sem=sem,
            device_id=sibling,
            device_id_type=MESH,
        ).wait_recv()

    def run_of(dz, core):
        return 2 * ((z + n_z - dz) % n_z) + core

    order = [0, 1, n_z - 1] + list(range(2, n_z - 1))
    for dz in order[:n_z]:
        group = kv_all.at[:, pl.ds(run_of(dz, c) * runs, runs)]
        await_bytes(group, kv_recv.at[dz])
        pltpu.make_async_remote_copy(
            src_ref=group,
            dst_ref=group,
            send_sem=pass_send.at[0],
            recv_sem=pass_recv.at[0],
            device_id=sibling,
            device_id_type=MESH,
        ).start()
    pltpu.make_async_copy(owner_in, owner_ref, owner_sem.at[0]).wait()
    await_bytes(qg_all, pass_recv.at[0])

    def contract(left, right, dims):
        return lax.dot_general(
            left, right, ((dims[:1], dims[1:]), ((), ())), preferred_element_type=jnp.float32
        )

    def query_step(z1, r):
        row = z1 * runs + r
        block = (2 * z1 + c) * runs + r
        low = (block + total_blocks - 1) % total_blocks
        high = (block + 1) % total_blocks
        picks = [owner_ref[j, block] * runs + r for j in range(PICKS)]
        named = [low, block, high] + picks + [0, 1]
        keys = jnp.concatenate([kv_all[0, n] for n in named], axis=0)
        values = jnp.concatenate([kv_all[1, n] for n in named], axis=0)
        query = qg_all[0, row]
        grad = qg_all[1, row]
        scores = contract(keys, query, (1, 1))
        top = jnp.max(scores, axis=0, keepdims=True)
        weights = jnp.exp((scores - top) * factor)
        weights = weights * (1.0 / jnp.sum(weights, axis=0, keepdims=True))
        rounded = weights.astype(jnp.bfloat16)
        grad_weights = contract(values, grad, (1, 1))
        delta = jnp.sum(weights * grad_weights, axis=0, keepdims=True)
        grad_scores = (weights * (grad_weights - delta) * factor).astype(jnp.bfloat16)
        stage[0, row] = contract(rounded, values, (0, 0)).astype(jnp.bfloat16)
        stage[1, row] = contract(grad_scores, keys, (0, 0)).astype(jnp.bfloat16)
        key_terms = contract(grad_scores, query, (1, 0))
        value_terms = contract(rounded, grad, (1, 0))
        for j, n in ((0, low), (1, block), (2, high), (6, 0), (7, 1)):
            k_sum[n] += key_terms[j * BLOCK : (j + 1) * BLOCK]
            v_sum[n] += value_terms[j * BLOCK : (j + 1) * BLOCK]
        for j in range(PICKS):
            rows = slice((3 + j) * BLOCK, (4 + j) * BLOCK)
            k_far[row * PICKS + j] = key_terms[rows].astype(jnp.bfloat16)
            v_far[row * PICKS + j] = value_terms[rows].astype(jnp.bfloat16)

    def hand_out(first, dz):
        z2 = (z + n_z - dz) % n_z
        source = stage.at[pl.ds(first, 2), pl.ds(z2 * runs, runs)]
        target = out.at[pl.ds(first, 2), :, :, columns(z)]
        if isinstance(dz, int) and dz == 0:
            pltpu.make_async_copy(source, target, out_recv.at[0]).start()
        else:
            pltpu.make_async_remote_copy(
                src_ref=source,
                dst_ref=target,
                send_sem=out_send.at[0],
                recv_sem=out_recv.at[0],
                device_id={"head": head, "blk": 2 * z2 + c},
                device_id_type=MESH,
            ).start()

    def await_sent(ref, sem):
        pltpu.make_async_remote_copy(
            src_ref=ref,
            dst_ref=ref,
            send_sem=sem,
            recv_sem=sem,
            device_id=sibling,
            device_id_type=MESH,
        ).wait_send()

    rows = n_z * runs
    far_first = [dz for dz in (2, 1, 3, 0) if dz < n_z] + list(range(4, n_z))
    for dz in far_first:
        z1 = (z + n_z - dz) % n_z
        await_bytes(qg_all.at[:, pl.ds(z1 * runs, runs)], qg_recv.at[dz])

        def step(r, carry, z1=z1):
            query_step(z1, r)
            return carry

        lax.fori_loop(0, runs, step, 0)
        if dz == far_first[0]:
            await_sent(kv_all.at[:, pl.ds(0, 2 * (rows - 1))], in_send.at[0])
        hand_out(0, dz)

    def total_of(sums, far, run, r):
        total = sums[run * runs + r]
        for z1 in range(n_z):
            block = (2 * z1 + c) * runs + r
            row = z1 * runs + r
            place = none
            for j in range(PICKS):
                place = jnp.where(owner_ref[j, block] == run, row * PICKS + j, place)
            total = total + far[place].astype(jnp.float32)
        return total

    def give_step(row, carry):
        run, r = 2 * (row // runs) + 1 - c, row % runs
        give[0, row] = total_of(k_sum, k_far, run, r).astype(jnp.bfloat16)
        give[1, row] = total_of(v_sum, v_far, run, r).astype(jnp.bfloat16)
        return carry

    lax.fori_loop(0, n_z * runs, give_step, 0)
    pair = pltpu.make_async_remote_copy(
        src_ref=give,
        dst_ref=take,
        send_sem=pair_send.at[0],
        recv_sem=pair_recv.at[0],
        device_id=sibling,
        device_id_type=MESH,
    )
    pair.start()
    pair.wait_recv()
    falling = list(range(n_z - 1, -1, -1))
    for below, above in zip(falling, far_first if n_z == 4 else falling):
        dz = jnp.where(z < n_z // 2, below, above) if below else 0
        z1 = (z + n_z - dz) % n_z

        def join_step(r, carry, z1=z1):
            row, run = z1 * runs + r, 2 * z1 + c
            for at, sums, far in ((0, k_sum, k_far), (1, v_sum, v_far)):
                total = total_of(sums, far, run, r) + take[at, row].astype(jnp.float32)
                stage[2 + at, row] = total.astype(jnp.bfloat16)
            return carry

        lax.fori_loop(0, runs, join_step, 0)
        hand_out(2, dz)

    pair.wait_send()
    await_sent(qg_all, pass_send.at[0])
    if n_z > 1:
        await_sent(kv_all.at[:, pl.ds(0, 2 * (rows - runs))], out_send.at[0])
    await_bytes(out, out_recv.at[0])


def settle_kernel(count, pieces, source, *refs):
    targets, sem = refs[:count], refs[count]
    copies = [
        pltpu.make_async_copy(
            source.at[at, piece], targets[at].at[piece], sem.at[0]
        )
        for at in range(count)
        for piece in range(pieces)
    ]
    for copy in copies:
        copy.start()
    pltpu.make_async_copy(source, source, sem.at[0]).wait()


def by_heads(queries, keys, values, grad_out, stride_owner):
    n_head, n_blk = lax.axis_size("head"), lax.axis_size("blk")
    n_z = n_blk // 2
    rows = n_z * n_head
    rounds = len(entry_rounds(n_head, n_z)[0])
    seq_rows, width = BLOCK * n_head, n_z * HEAD_DIM
    tile = (BLOCK, HEAD_DIM)
    low, wide = jnp.bfloat16, jnp.float32
    dma = pltpu.SemaphoreType.DMA
    out_bytes = 8 * seq_rows * width
    arrived = pl.pallas_call(
        partial(head_kernel, n_head, n_z),
        out_shape=pltpu.VMEM((4, n_head, BLOCK, width), low),
        in_specs=[pl.BlockSpec(memory_space=pltpu.HBM)] * 5,
        out_specs=pl.BlockSpec(memory_space=pltpu.VMEM),
        scratch_shapes=[
            pltpu.SMEM(stride_owner.shape[::-1], jnp.int32),
            pltpu.VMEM((2, 2 * rows) + tile, low),
            pltpu.VMEM((2, rows) + tile, low),
            pltpu.VMEM((2 * rows,) + tile, wide),
            pltpu.VMEM((2 * rows,) + tile, wide),
            pltpu.VMEM((rows * PICKS + 1,) + tile, low),
            pltpu.VMEM((rows * PICKS + 1,) + tile, low),
            pltpu.VMEM((4, rows) + tile, low),
            pltpu.VMEM((2, rows) + tile, low),
            pltpu.VMEM((2, rows) + tile, low),
            dma((1,)),
            dma((1,)),
            dma((n_z,)),
            dma((n_z,)),
            dma((1,)),
            dma((1,)),
            dma((1,)),
            dma((1,)),
            dma((1,)),
            dma((1,)),
            pltpu.SemaphoreType.REGULAR((max(1, rounds - 1),)),
        ],
        compiler_params=pltpu.CompilerParams(
            collective_id=0, has_side_effects=True, vmem_limit_bytes=67043328 - out_bytes
        ),
    )(stride_owner.T, queries, keys, values, grad_out)
    out = jax.ShapeDtypeStruct((n_head, BLOCK, width), low)
    settled = pl.pallas_call(
        partial(settle_kernel, 4, n_head),
        out_shape=(out,) * 4,
        in_specs=[pl.BlockSpec(memory_space=pltpu.VMEM)],
        out_specs=(pl.BlockSpec(memory_space=pl.ANY),) * 4,
        scratch_shapes=[dma((1,))],
        compiler_params=pltpu.CompilerParams(vmem_limit_bytes=8 << 20),
    )(arrived)
    return tuple(part.reshape(seq_rows, width) for part in settled)


def on_device(queries, keys, values, grad_out, stride_owner):
    n_head, n_blk = lax.axis_size("head"), lax.axis_size("blk")
    rows, width = queries.shape
    whole_heads = n_blk % 2 == 0 and width == n_head * (n_blk // 2) * HEAD_DIM
    if rows == BLOCK and whole_heads and n_head & (n_head - 1) == 0:
        return by_heads(queries, keys, values, grad_out, stride_owner)
    return by_runs(queries, keys, values, grad_out, stride_owner)


def solution(mesh):
    return jax.shard_map(
        on_device,
        mesh=mesh,
        in_specs=(
            P(("blk", "head"), None),
            P(("blk", "head"), None),
            P(("blk", "head"), None),
            P(("blk", "head"), None),
            P(),
        ),
        out_specs=(P("blk", "head"), P("blk", "head"), P("blk", "head"), P("blk", "head")),
        check_vma=False,
    )
```

```python
import math
from functools import partial

import jax
import jax.numpy as jnp
from jax import lax
from jax.experimental import pallas as pl
from jax.experimental.pallas import tpu as pltpu
from jax.sharding import PartitionSpec as P

HEAD_DIM = 128
BLOCK = 128
PICKS = 3
MESH = pl.DeviceIdType.MESH


def with_halo(block, sides, width):
    for axis, dim in sides:
        count = lax.axis_size(axis)
        forward = [(i, i + 1) for i in range(count - 1)]
        forward.append((count - 1, 0))
        backward = [(target, source) for source, target in forward]
        low = lax.ppermute(
            lax.slice_in_dim(block, block.shape[dim] - width, None, axis=dim), axis, forward
        )
        high = lax.ppermute(lax.slice_in_dim(block, 0, width, axis=dim), axis, backward)
        block = jnp.concatenate([low, block, high], axis=dim)
    return block


def from_root(block, axis, holder):
    block = jnp.where(lax.axis_index(axis) == holder, block, jnp.zeros_like(block))
    return lax.psum(block, axis)


def slot_tables(stride_owner, n_blk, blocks, capacity, device):
    owner_table = stride_owner.reshape(n_blk, blocks, PICKS)
    owner_ids = jnp.arange(n_blk, dtype=jnp.int32)
    naming = jnp.any(owner_table[:, :, :, None] == owner_ids[None, None, None, :], axis=2)
    counts = naming.astype(jnp.int32)
    ranking = jnp.cumsum(counts, axis=1) - counts
    naming_here = lax.dynamic_index_in_dim(naming, device, 2, keepdims=False)
    ranking_here = lax.dynamic_index_in_dim(ranking, device, 2, keepdims=False)
    slot_ids = jnp.arange(capacity, dtype=jnp.int32)
    matched = naming_here[:, None, :] & (ranking_here[:, None, :] == slot_ids[None, :, None])
    offsets = jnp.sum(
        matched.astype(jnp.int32) * jnp.arange(blocks, dtype=jnp.int32)[None, None, :], axis=2
    )
    own_rows = lax.dynamic_index_in_dim(owner_table, device, 0, keepdims=False)
    own_ranks = lax.dynamic_index_in_dim(ranking, device, 0, keepdims=False)
    picked = jnp.take_along_axis(own_ranks, own_rows, axis=1)
    flat_slot = own_rows * capacity + picked
    return (offsets.reshape(-1), flat_slot, matched.reshape(n_blk * capacity, blocks))


def fetch_keys(stacked, offsets, flat_slot, capacity):
    seq_rows = stacked.shape[1]
    width = stacked.shape[2]
    blocks = seq_rows // BLOCK
    n_blk = lax.axis_size("blk")
    extended = with_halo(stacked, (("blk", 1),), BLOCK)
    extended = extended.reshape(2, blocks + 2, BLOCK, width)
    block_view = stacked.reshape(2, blocks, BLOCK, width)
    leading = from_root(block_view[:, 0:2], "blk", 0)
    outgoing = jnp.take(block_view, offsets, axis=1).reshape(2, n_blk, capacity, BLOCK, width)
    incoming = lax.all_to_all(outgoing, "blk", split_axis=1, concat_axis=1, tiled=True)
    incoming = incoming.reshape(2, n_blk * capacity, BLOCK, width)
    pooled = jnp.concatenate([extended, incoming, leading], axis=1)
    rows_here = jnp.arange(blocks, dtype=jnp.int32)[:, None]
    nearby_index = rows_here + jnp.arange(3, dtype=jnp.int32)[None, :]
    distant_index = blocks + 2 + flat_slot
    leading_index = (
        jnp.zeros((blocks, 2), jnp.int32)
        + (blocks + 2 + n_blk * capacity)
        + jnp.arange(2, dtype=jnp.int32)[None, :]
    )
    table = jnp.concatenate([nearby_index, distant_index, leading_index], axis=1)
    return jnp.take(pooled, table.reshape(-1), axis=1)


def score_block(query_part, key_part, factor):
    return (
        jnp.einsum("gqhd,gjkhd->ghqjk", query_part, key_part, preferred_element_type=jnp.float32)
        * factor
    )


def log_normal(scores):
    row_max = jnp.max(scores, axis=(3, 4), keepdims=True)
    return row_max + jnp.log(jnp.sum(jnp.exp(scores - row_max), axis=(3, 4), keepdims=True))


def output_of(rounded, value_part):
    return jnp.einsum(
        "ghqjk,gjkhd->gqhd", rounded, value_part, preferred_element_type=jnp.float32
    ).astype(jnp.bfloat16)


def split_terms(coeffs, source):
    group_size = source.shape[0]
    near = jnp.einsum(
        "ghqjk,gqhd->gjkhd", coeffs[:, :, :, 0:3], source, preferred_element_type=jnp.float32
    )
    far = jnp.einsum(
        "ghqjk,gqhd->gjkhd", coeffs[:, :, :, 3:6], source, preferred_element_type=jnp.float32
    ).astype(jnp.bfloat16)
    lead = jnp.einsum(
        "ghqjk,gqhd->jkhd", coeffs[:, :, :, 6:8], source, preferred_element_type=jnp.float32
    )
    near = near.reshape(group_size, 3, near.shape[2], near.shape[3] * near.shape[4])
    far = far.reshape(group_size, 3, far.shape[2], far.shape[3] * far.shape[4])
    lead = lead.reshape(2, lead.shape[1], lead.shape[2] * lead.shape[3])
    return (near, far, lead)


def backward_from(
    scores, log_total, rounded, attended, grad_part, query_part, key_part, value_part, factor
):
    grad_weights = jnp.einsum(
        "gqhd,gjkhd->ghqjk", grad_part, value_part, preferred_element_type=jnp.float32
    )
    delta = jnp.sum(grad_part.astype(jnp.float32) * attended.astype(jnp.float32), axis=3)
    delta = jnp.transpose(delta, (0, 2, 1))[:, :, :, None, None]
    grad_scores = (jnp.exp(scores - log_total) * (grad_weights - delta) * factor).astype(
        jnp.bfloat16
    )
    grad_query = jnp.einsum(
        "ghqjk,gjkhd->gqhd", grad_scores, key_part, preferred_element_type=jnp.float32
    ).astype(jnp.bfloat16)
    key_near, key_far, key_lead = split_terms(grad_scores, query_part)
    value_near, value_far, value_lead = split_terms(rounded, grad_part)
    return (grad_query, key_near, key_far, key_lead, value_near, value_far, value_lead)


def spread_near(near_terms, width):
    blank = jnp.zeros((1, BLOCK, width), jnp.float32)
    return (
        jnp.concatenate([near_terms[:, 0], blank, blank], axis=0)
        + jnp.concatenate([blank, near_terms[:, 1], blank], axis=0)
        + jnp.concatenate([blank, blank, near_terms[:, 2]], axis=0)
    )


def by_runs(queries, keys, values, grad_out, stride_owner):
    query_rows, key_rows, value_rows, grad_rows = (
        lax.all_to_all(queries, "head", split_axis=1, concat_axis=0, tiled=True),
        lax.all_to_all(keys, "head", split_axis=1, concat_axis=0, tiled=True),
        lax.all_to_all(values, "head", split_axis=1, concat_axis=0, tiled=True),
        lax.all_to_all(grad_out, "head", split_axis=1, concat_axis=0, tiled=True),
    )
    seq_rows, width = query_rows.shape
    heads_here = width // HEAD_DIM
    blocks = seq_rows // BLOCK
    n_blk = lax.axis_size("blk")
    capacity = max(2, (PICKS * blocks + n_blk - 1) // n_blk)
    device = lax.axis_index("blk")
    offsets, flat_slot, matched = slot_tables(stride_owner, n_blk, blocks, capacity, device)
    group_size = math.gcd(blocks, max(1, 512 // BLOCK))
    group_count = blocks // group_size
    factor = HEAD_DIM ** (-0.5)
    stacked = jnp.stack([key_rows, value_rows])
    query_view = query_rows.reshape(blocks, BLOCK, heads_here, HEAD_DIM)
    grad_view = grad_rows.reshape(blocks, BLOCK, heads_here, HEAD_DIM)
    key_sets = fetch_keys(stacked, offsets, flat_slot, capacity)
    key_sets = key_sets.reshape(2, blocks, 8, BLOCK, heads_here, HEAD_DIM)

    def pieces(group_id):
        start = group_id * group_size
        query_part = lax.dynamic_slice_in_dim(query_view, start, group_size, 0)
        grad_part = lax.dynamic_slice_in_dim(grad_view, start, group_size, 0)
        kv_part = lax.dynamic_slice_in_dim(key_sets, start, group_size, 1)
        return (query_part, grad_part, kv_part[0], kv_part[1])

    def joined_pass(group_id):
        query_part, grad_part, key_part, value_part = pieces(group_id)
        scores = score_block(query_part, key_part, factor)
        log_total = log_normal(scores)
        rounded = jnp.exp(scores - log_total).astype(jnp.bfloat16)
        attended = output_of(rounded, value_part)
        extra = backward_from(
            scores,
            log_total,
            rounded,
            attended,
            grad_part,
            query_part,
            key_part,
            value_part,
            factor,
        )
        return (attended,) + extra

    group_ids = jnp.arange(group_count, dtype=jnp.int32)
    results = lax.map(joined_pass, group_ids)
    attended = results[0]
    grad_query, key_near, key_far, key_lead, value_near, value_far, value_lead = results[1:]
    key_ext = spread_near(key_near.reshape(blocks, 3, BLOCK, width), width)
    value_ext = spread_near(value_near.reshape(blocks, 3, BLOCK, width), width)
    rim_terms = jnp.stack(
        [
            jnp.stack([key_ext[0], value_ext[0]]),
            jnp.stack([key_ext[blocks + 1], value_ext[blocks + 1]]),
        ]
    )
    beside = with_halo(rim_terms.astype(jnp.bfloat16), (("blk", 0),), 1).astype(rim_terms.dtype)
    key_owned = key_ext[1 : blocks + 1].at[0].add(beside[0, 0]).at[blocks - 1].add(beside[3, 0])
    value_owned = value_ext[1 : blocks + 1].at[0].add(beside[0, 1]).at[blocks - 1].add(beside[3, 1])
    slot_flat = flat_slot.reshape(-1)
    key_back = (
        jnp.zeros((n_blk * capacity, BLOCK, width), jnp.bfloat16)
        .at[slot_flat]
        .set(key_far.reshape(blocks * PICKS, BLOCK, width))
    )
    value_back = (
        jnp.zeros((n_blk * capacity, BLOCK, width), jnp.bfloat16)
        .at[slot_flat]
        .set(value_far.reshape(blocks * PICKS, BLOCK, width))
    )
    key_arrived, value_arrived = (
        lax.all_to_all(
            key_back.reshape(n_blk, capacity, BLOCK, width),
            "blk",
            split_axis=0,
            concat_axis=0,
            tiled=True,
        ),
        lax.all_to_all(
            value_back.reshape(n_blk, capacity, BLOCK, width),
            "blk",
            split_axis=0,
            concat_axis=0,
            tiled=True,
        ),
    )
    match_b = matched.astype(jnp.bfloat16)
    key_owned = key_owned + jnp.einsum(
        "sr,sbc->rbc",
        match_b,
        key_arrived.reshape(n_blk * capacity, BLOCK, width),
        preferred_element_type=jnp.float32,
    )
    value_owned = value_owned + jnp.einsum(
        "sr,sbc->rbc",
        match_b,
        value_arrived.reshape(n_blk * capacity, BLOCK, width),
        preferred_element_type=jnp.float32,
    )
    key_total, value_total = (
        lax.psum(jnp.sum(key_lead, axis=0).astype(jnp.bfloat16), "blk").astype(jnp.float32),
        lax.psum(jnp.sum(value_lead, axis=0).astype(jnp.bfloat16), "blk").astype(jnp.float32),
    )
    at_root = device == 0
    key_owned = key_owned.at[0:2].add(jnp.where(at_root, key_total, jnp.zeros_like(key_total)))
    value_owned = value_owned.at[0:2].add(
        jnp.where(at_root, value_total, jnp.zeros_like(value_total))
    )
    grad_keys = key_owned.astype(jnp.bfloat16).reshape(seq_rows, width)
    grad_values = value_owned.astype(jnp.bfloat16).reshape(seq_rows, width)
    return (
        attended.reshape(seq_rows, width),
        grad_query.reshape(seq_rows, width),
        grad_keys,
        grad_values,
    )


def head_bits(n_head):
    return [1 << bit for bit in range(n_head.bit_length() - 1)]


def neighbours(n_head, n_z, at_z):
    beside = [(at_z, flip, 0) for flip in head_bits(n_head)] + [(at_z, 0, 1)]
    return beside + [(z2, 0, 0) for z2 in (at_z - 1, at_z + 1) if 0 <= z2 < n_z]


def seen_from(peer, at_z):
    return (at_z, peer[1], peer[2])


def entry_rounds(n_head, n_z):
    middle = n_z // 2
    hears, knows = [], []
    near = [neighbours(n_head, n_z, at_z) for at_z in range(n_z)]
    first = [set(near[at_z]) for at_z in range(n_z)]
    if middle:
        first[middle] = {(middle - 1, 0, 0)}
    hears.append(first)
    knows.append([{(at_z, 0, 0)} | first[at_z] for at_z in range(n_z)])
    reached = [
        {(z2, flips, 0) for z2 in range(n_z) for flips in range(n_head)} | {(at_z, 0, 1)}
        for at_z in range(n_z)
    ]
    while any(want - known for want, known in zip(reached, knows[-1])):
        known = knows[-1]
        heard = [
            {p for p in near[at_z] if seen_from(p, at_z) in known[p[0]]} for at_z in range(n_z)
        ]
        hears.append(heard)
        knows.append(
            [
                known[at_z].union(
                    *(
                        {(k[0], k[1] ^ p[1], k[2] ^ p[2]) for k in known[p[0]]}
                        for p in heard[at_z]
                    )
                )
                for at_z in range(n_z)
            ]
        )
    return hears, knows


def head_kernel(
    n_head,
    n_z,
    owner_in,
    q_in,
    k_in,
    v_in,
    g_in,
    out,
    owner_ref,
    kv_all,
    qg_all,
    k_sum,
    v_sum,
    k_far,
    v_far,
    stage,
    give,
    take,
    owner_sem,
    in_send,
    kv_recv,
    qg_recv,
    pass_send,
    pass_recv,
    pair_recv,
    out_send,
    out_recv,
    near_sem,
):
    head = lax.axis_index("head")
    blk = lax.axis_index("blk")
    z = blk // 2
    c = blk % 2
    runs = n_head
    total_blocks = 2 * n_z * runs
    factor = HEAD_DIM ** (-0.5)
    my_head = head * n_z + z
    mine = blk * runs + head
    my_row = z * runs + head
    sibling = {"head": head, "blk": 2 * z + 1 - c}

    def columns(head_id):
        return pl.ds(pl.multiple_of(head_id * HEAD_DIM, HEAD_DIM), HEAD_DIM)

    bits = head_bits(n_head)
    hears, knows = entry_rounds(n_head, n_z)
    barrier = pltpu.get_barrier_semaphore()

    def flipped(flips):
        moved = head
        for flip in bits:
            if flips & flip:
                moved = moved + flip - 2 * flip * ((head // flip) % 2)
        return moved

    def place(peer):
        at_z, flips, other = peer
        return {"head": flipped(flips), "blk": 2 * at_z + (1 - c if other else c)}

    def greet(at_z, step):
        sem = barrier if step == 0 else near_sem.at[step - 1]
        for peer in neighbours(n_head, n_z, at_z):
            if seen_from(peer, at_z) in hears[step][peer[0]]:
                pl.semaphore_signal(sem, inc=1, device_id=place(peer), device_id_type=MESH)

    def hear(at_z, step):
        sem = barrier if step == 0 else near_sem.at[step - 1]
        if hears[step][at_z]:
            pl.semaphore_wait(sem, len(hears[step][at_z]))

    def push(sources, target, slot, recv_sem, at_z, peer):
        z2, flips, _ = peer
        for at, source in enumerate(sources):
            pltpu.make_async_remote_copy(
                src_ref=source.at[:, columns(flipped(flips) * n_z + z2)],
                dst_ref=target.at[at, slot],
                send_sem=in_send.at[0],
                recv_sem=recv_sem.at[(z2 + n_z - at_z) % n_z],
                device_id=place(peer),
                device_id_type=MESH,
            ).start()

    def crosses(at_z, peer):
        return (at_z < n_z // 2) != (peer[0] < n_z // 2)

    def urgency(at_z, peer):
        hops = abs(peer[0] - at_z) + bin(peer[1]).count("1")
        return (not crosses(at_z, peer), hops, peer)

    def enter(at_z):
        greet(at_z, 0)
        local = [pltpu.make_async_copy(owner_in, owner_ref, owner_sem.at[0])]
        for sources, target, slot, sem in (
            ((k_in, v_in), kv_all, mine, kv_recv),
            ((q_in, g_in), qg_all, my_row, qg_recv),
        ):
            for at, source in enumerate(sources):
                local.append(
                    pltpu.make_async_copy(
                        source.at[:, columns(my_head)], target.at[at, slot], sem.at[0]
                    )
                )
        for copy in local:
            copy.start()
        early = []
        met = {(at_z, 0, 0)}
        for step in range(len(hears)):
            hear(at_z, step)
            fresh = [p for p in knows[step][at_z] - met if not p[2]]
            met |= knows[step][at_z]
            fresh.sort(key=partial(urgency, at_z))
            first = [p for p in fresh if step == 0 and crosses(at_z, p)]
            for peer in first:
                push((k_in, v_in), kv_all, mine, kv_recv, at_z, peer)
                push((q_in, g_in), qg_all, my_row, qg_recv, at_z, peer)
            early += first
            if step + 1 < len(hears):
                greet(at_z, step + 1)
            for peer in fresh:
                if peer not in first:
                    push((k_in, v_in), kv_all, mine, kv_recv, at_z, peer)
        late = [p for p in met if not p[2] and p[:2] != (at_z, 0) and p not in early]
        for dz in [n_z // 2] + [d for d in range(n_z - 1, -1, -1) if d != n_z // 2]:
            for peer in sorted(late, key=partial(urgency, at_z)):
                if abs(peer[0] - at_z) == dz:
                    push((q_in, g_in), qg_all, my_row, qg_recv, at_z, peer)

    for at_z in range(n_z):
        pl.when(z == at_z)(partial(enter, at_z))

    blank = jnp.zeros((BLOCK, HEAD_DIM), jnp.float32)

    def clear(n, carry):
        k_sum[n] = blank
        v_sum[n] = blank
        return carry

    lax.fori_loop(0, total_blocks, clear, 0)
    none = n_z * runs * PICKS
    k_far[none] = blank.astype(jnp.bfloat16)
    v_far[none] = blank.astype(jnp.bfloat16)

    def await_bytes(ref, sem):
        pltpu.make_async_remote_copy(
            src_ref=ref,
            dst_ref=ref,
            send_sem=sem,
            recv_sem=sem,
            device_id=sibling,
            device_id_type=MESH,
        ).wait_recv()

    def run_of(dz, core):
        return 2 * ((z + n_z - dz) % n_z) + core

    order = [0, 1, n_z - 1] + list(range(2, n_z - 1))
    for dz in order[:n_z]:
        group = kv_all.at[:, pl.ds(run_of(dz, c) * runs, runs)]
        await_bytes(group, kv_recv.at[dz])
        pltpu.make_async_remote_copy(
            src_ref=group,
            dst_ref=group,
            send_sem=pass_send.at[0],
            recv_sem=pass_recv.at[0],
            device_id=sibling,
            device_id_type=MESH,
        ).start()
    pltpu.make_async_copy(owner_in, owner_ref, owner_sem.at[0]).wait()
    await_bytes(qg_all, pass_recv.at[0])

    def contract(left, right, dims):
        return lax.dot_general(
            left, right, ((dims[:1], dims[1:]), ((), ())), preferred_element_type=jnp.float32
        )

    def query_step(z1, r):
        row = z1 * runs + r
        block = (2 * z1 + c) * runs + r
        low = (block + total_blocks - 1) % total_blocks
        high = (block + 1) % total_blocks
        picks = [owner_ref[j, block] * runs + r for j in range(PICKS)]
        named = [low, block, high] + picks + [0, 1]
        keys = jnp.concatenate([kv_all[0, n] for n in named], axis=0)
        values = jnp.concatenate([kv_all[1, n] for n in named], axis=0)
        query = qg_all[0, row]
        grad = qg_all[1, row]
        scores = contract(keys, query, (1, 1))
        top = jnp.max(scores, axis=0, keepdims=True)
        weights = jnp.exp((scores - top) * factor)
        weights = weights * (1.0 / jnp.sum(weights, axis=0, keepdims=True))
        rounded = weights.astype(jnp.bfloat16)
        grad_weights = contract(values, grad, (1, 1))
        delta = jnp.sum(weights * grad_weights, axis=0, keepdims=True)
        grad_scores = (weights * (grad_weights - delta) * factor).astype(jnp.bfloat16)
        stage[0, row] = contract(rounded, values, (0, 0)).astype(jnp.bfloat16)
        stage[1, row] = contract(grad_scores, keys, (0, 0)).astype(jnp.bfloat16)
        key_terms = contract(grad_scores, query, (1, 0))
        value_terms = contract(rounded, grad, (1, 0))
        for j, n in ((0, low), (1, block), (2, high), (6, 0), (7, 1)):
            k_sum[n] += key_terms[j * BLOCK : (j + 1) * BLOCK]
            v_sum[n] += value_terms[j * BLOCK : (j + 1) * BLOCK]
        for j in range(PICKS):
            rows = slice((3 + j) * BLOCK, (4 + j) * BLOCK)
            k_far[row * PICKS + j] = key_terms[rows].astype(jnp.bfloat16)
            v_far[row * PICKS + j] = value_terms[rows].astype(jnp.bfloat16)

    def hand_out(first, dz):
        z2 = (z + n_z - dz) % n_z
        source = stage.at[pl.ds(first, 2), pl.ds(z2 * runs, runs)]
        target = out.at[pl.ds(first, 2), :, :, columns(z)]
        if isinstance(dz, int) and dz == 0:
            pltpu.make_async_copy(source, target, out_recv.at[0]).start()
        else:
            pltpu.make_async_remote_copy(
                src_ref=source,
                dst_ref=target,
                send_sem=out_send.at[0],
                recv_sem=out_recv.at[0],
                device_id={"head": head, "blk": 2 * z2 + c},
                device_id_type=MESH,
            ).start()

    def await_sent(ref, sem):
        pltpu.make_async_remote_copy(
            src_ref=ref,
            dst_ref=ref,
            send_sem=sem,
            recv_sem=sem,
            device_id=sibling,
            device_id_type=MESH,
        ).wait_send()

    rows = n_z * runs
    far_first = [dz for dz in (2, 1, 3, 0) if dz < n_z] + list(range(4, n_z))
    for dz in far_first:
        z1 = (z + n_z - dz) % n_z
        await_bytes(qg_all.at[:, pl.ds(z1 * runs, runs)], qg_recv.at[dz])

        def step(r, carry, z1=z1):
            query_step(z1, r)
            return carry

        lax.fori_loop(0, runs, step, 0)
        if dz == far_first[0]:
            await_sent(kv_all.at[:, pl.ds(0, 2 * (rows - 1))], in_send.at[0])
        hand_out(0, dz)

    def total_of(sums, far, run, r):
        total = sums[run * runs + r]
        for z1 in range(n_z):
            block = (2 * z1 + c) * runs + r
            row = z1 * runs + r
            place = none
            for j in range(PICKS):
                place = jnp.where(owner_ref[j, block] == run, row * PICKS + j, place)
            total = total + far[place].astype(jnp.float32)
        return total

    def give_step(row, carry):
        run, r = 2 * (row // runs) + 1 - c, row % runs
        give[0, row] = total_of(k_sum, k_far, run, r).astype(jnp.bfloat16)
        give[1, row] = total_of(v_sum, v_far, run, r).astype(jnp.bfloat16)
        return carry

    lax.fori_loop(0, n_z * runs, give_step, 0)
    pair = pltpu.make_async_remote_copy(
        src_ref=give,
        dst_ref=take,
        send_sem=pass_send.at[0],
        recv_sem=pair_recv.at[0],
        device_id=sibling,
        device_id_type=MESH,
    )
    pair.start()
    pair.wait_recv()
    falling = list(range(n_z - 1, -1, -1))
    for below, above in zip(falling, far_first if n_z == 4 else falling):
        dz = jnp.where(z < n_z // 2, below, above) if below else 0
        z1 = (z + n_z - dz) % n_z

        def join_step(r, carry, z1=z1):
            row, run = z1 * runs + r, 2 * z1 + c
            for at, sums, far in ((0, k_sum, k_far), (1, v_sum, v_far)):
                total = total_of(sums, far, run, r) + take[at, row].astype(jnp.float32)
                stage[2 + at, row] = total.astype(jnp.bfloat16)
            return carry

        lax.fori_loop(0, runs, join_step, 0)
        hand_out(2, dz)

    await_sent(kv_all, pass_send.at[0])
    if n_z > 1:
        await_sent(kv_all.at[:, pl.ds(0, 2 * (rows - runs))], out_send.at[0])
    await_bytes(out, out_recv.at[0])


def settle_kernel(count, pieces, source, *refs):
    targets, sem = refs[:count], refs[count]
    copies = [
        pltpu.make_async_copy(
            source.at[at, piece], targets[at].at[piece], sem.at[0]
        )
        for at in range(count)
        for piece in range(pieces)
    ]
    for copy in copies:
        copy.start()
    pltpu.make_async_copy(source, source, sem.at[0]).wait()


def by_heads(queries, keys, values, grad_out, stride_owner):
    n_head, n_blk = lax.axis_size("head"), lax.axis_size("blk")
    n_z = n_blk // 2
    rows = n_z * n_head
    seq_rows, width = BLOCK * n_head, n_z * HEAD_DIM
    tile = (BLOCK, HEAD_DIM)
    low, wide = jnp.bfloat16, jnp.float32
    dma = pltpu.SemaphoreType.DMA
    rounds = len(entry_rounds(n_head, n_z)[0])
    out_bytes = 8 * seq_rows * width
    arrived = pl.pallas_call(
        partial(head_kernel, n_head, n_z),
        out_shape=pltpu.VMEM((4, n_head, BLOCK, width), low),
        in_specs=[pl.BlockSpec(memory_space=pltpu.HBM)] * 5,
        out_specs=pl.BlockSpec(memory_space=pltpu.VMEM),
        scratch_shapes=[
            pltpu.SMEM(stride_owner.shape[::-1], jnp.int32),
            pltpu.VMEM((2, 2 * rows) + tile, low),
            pltpu.VMEM((2, rows) + tile, low),
            pltpu.VMEM((2 * rows,) + tile, wide),
            pltpu.VMEM((2 * rows,) + tile, wide),
            pltpu.VMEM((rows * PICKS + 1,) + tile, low),
            pltpu.VMEM((rows * PICKS + 1,) + tile, low),
            pltpu.VMEM((4, rows) + tile, low),
            pltpu.VMEM((2, rows) + tile, low),
            pltpu.VMEM((2, rows) + tile, low),
            dma((1,)),
            dma((1,)),
            dma((n_z,)),
            dma((n_z,)),
            dma((1,)),
            dma((1,)),
            dma((1,)),
            dma((1,)),
            dma((1,)),
            pltpu.SemaphoreType.REGULAR((max(1, rounds - 1),)),
        ],
        compiler_params=pltpu.CompilerParams(
            collective_id=0, has_side_effects=True, vmem_limit_bytes=67043328 - out_bytes
        ),
    )(stride_owner.T, queries, keys, values, grad_out)
    out = jax.ShapeDtypeStruct((n_head, BLOCK, width), low)
    settled = pl.pallas_call(
        partial(settle_kernel, 4, n_head),
        out_shape=(out,) * 4,
        in_specs=[pl.BlockSpec(memory_space=pltpu.VMEM)],
        out_specs=(pl.BlockSpec(memory_space=pl.ANY),) * 4,
        scratch_shapes=[dma((1,))],
        compiler_params=pltpu.CompilerParams(vmem_limit_bytes=8 << 20),
    )(arrived)
    return tuple(part.reshape(seq_rows, width) for part in settled)


def on_device(queries, keys, values, grad_out, stride_owner):
    n_head, n_blk = lax.axis_size("head"), lax.axis_size("blk")
    rows, width = queries.shape
    whole_heads = n_blk % 2 == 0 and width == n_head * (n_blk // 2) * HEAD_DIM
    if rows == BLOCK and whole_heads and n_head & (n_head - 1) == 0:
        return by_heads(queries, keys, values, grad_out, stride_owner)
    return by_runs(queries, keys, values, grad_out, stride_owner)


def solution(mesh):
    return jax.shard_map(
        on_device,
        mesh=mesh,
        in_specs=(
            P(("blk", "head"), None),
            P(("blk", "head"), None),
            P(("blk", "head"), None),
            P(("blk", "head"), None),
            P(),
        ),
        out_specs=(P("blk", "head"), P("blk", "head"), P("blk", "head"), P("blk", "head")),
        check_vma=False,
    )
```
